32 devices in a mesh: slab: 8 (over y, x, core), pencil: 4 (over z).
Axes of the slice: x: 2, y: 2, z: 4, core: 2. Of those that a mesh axis runs over, the one named last changes fastest.
Arguments:
- template: float32 [256, 256, 256], P('slab', 'pencil'), may hold values from -6 to 6
- fixed_image: float32 [256, 256, 256], P('slab', 'pencil'), may hold values from -6 to 6
- velocity: float32 [3, 256, 256, 256], P(None, 'slab', 'pencil'), may hold values from -2 to 2
- src_owner: int32 [512, 2], P(('slab', 'pencil')), may hold values from 0 to 7, all different within a row; in each aligned block of 16 rows (0 to 15, 16 to 31, ...) at most 4 rows name the same one
- src_local: int32 [512, 2], P(('slab', 'pencil')), may hold values from 0 to 15
- weights: float32 [512, 2], P(('slab', 'pencil')), may hold values from 0.2 to 1
Outputs:
- gradient: float32 [3, 256, 256, 256], P(None, 'slab', 'pencil')
The draws below stay inside these ranges and needn't reach their ends.
Inputs may be any that keep to these rules, and one draw needn't show every extreme that they name: `src_owner`: within the 16 rows of one device no owner is named more than 4 times, a bound that some block reaches; each row names 2 different owners.
All inputs are finite; a program needn't handle non-finite values.
Results may differ from the reference program's by a relative error of at most 0.00007.
Values sent between devices are 32-bit elements; how exact they have to be, the bound alone decides.
A program may use at most 192 MiB of HBM per device.

```python
import math
import jax
import jax.numpy as jnp
import numpy as np

BZ = 32
BY = 64
NX = 256
BZB = 32
BYB = 32
BXB = 32
K = 2
BRICK = 32768
NB = 16
C = 4
NZ = 256
NY = 256
N_SLAB = 8
N_PENCIL = 4


def plant(values, stream_key, low, top_value):
    index_at = [jax.random.randint(jax.random.fold_in(stream_key, axis), (), 0, length) for axis, length in enumerate(values.shape)]
    longest = values.shape.index(max(values.shape))
    next_to = index_at[:longest] + [(index_at[longest] + 1) % values.shape[longest]] + index_at[longest + 1:]
    return values.at[tuple(index_at)].set(low).at[tuple(next_to)].set(top_value)


def block_scale(rng, dims, split, least, top_value):
    def one(axis_at, parts):
        heights = jax.random.uniform(jax.random.fold_in(jax.random.fold_in(rng, 6), axis_at), (parts,), jnp.float32, least / len(split), top_value / len(split))
        return jnp.repeat(jnp.exp(heights), dims[axis_at] // parts).reshape((-1,) + (1,) * (len(dims) - axis_at - 1))

    factor_of = one(*split[0])
    for cut in split[1:]:
        factor_of = factor_of * one(*cut)
    return factor_of


def deal_out(stream_key, own, number, rows, amount, top, reach, slope):
    ranking = jax.random.permutation(stream_key, amount)
    heavy_load, ordinary = portions_of(amount, rows * top, reach, slope, True), portions_of(amount, rows * top, reach, slope, False)
    places = jnp.arange(amount)

    def named(lengths, offset_by):
        used = int((lengths > 0).sum())
        fixed = max(1, used // 4)
        moved = fixed + (places - fixed + offset_by * (used - fixed)) % max(1, amount - fixed)
        return jnp.zeros((amount,), jnp.int32).at[ranking[jnp.where(places < fixed, places, moved)]].set(jnp.asarray(lengths, jnp.int32))

    lengths = jnp.where(number % 4 == 0, named(heavy_load, number // 4), named(ordinary, number - number // 4 - 1))
    mixed = jax.random.permutation(jax.random.fold_in(own, 3), amount)
    source_of, receiver = mixed[0:amount // 2 * 2:2], mixed[1:amount // 2 * 2:2]
    margin = jnp.minimum(lengths[source_of] - 1, reach - lengths[receiver]) // 2
    margin = jnp.where((source_of == ranking[0]) | (receiver == ranking[0]) | (lengths[receiver] == 0), 0, jnp.maximum(margin, 0))
    moved = jax.random.randint(jax.random.fold_in(own, 4), (amount // 2,), 0, 1 << 20) % (margin + 1)
    lengths = lengths.at[source_of].add(-moved).at[receiver].add(moved)
    items = jnp.searchsorted(jnp.cumsum(lengths), jnp.arange(rows * top), side="right").astype(jnp.int32)
    listing = items.reshape(top, rows).T
    listing = listing[jax.random.permutation(jax.random.fold_in(own, 1), rows)]
    offset_by = jax.random.randint(jax.random.fold_in(own, 2), (rows, 1), 0, top)
    return jnp.take_along_axis(listing, (jnp.arange(top)[None, :] + offset_by) % top, axis=1)


def portions_of(count, total, bound, skew, full):
    loads = [(1 << 20) // math.isqrt(standing ** skew) + 1 for standing in range(1, count + 1)]
    largest = bound if full else min(bound, max(-(-total // count), total * loads[0] // sum(loads)))
    least = 1 if total - largest >= count - 1 else 0
    counts, surplus = [largest] + [least] * (count - 1), total - largest - least * (count - 1)
    while surplus > 0:
        movable = [i for i in range(1, count) if counts[i] < largest] or [i for i in range(1, count) if counts[i] < bound]
        mass, remaining = sum([loads[i] for i in movable]), surplus
        for i in movable:
            addition = min(bound - counts[i], max(1, remaining * loads[i] // mass), surplus)
            counts[i] = counts[i] + addition
            surplus = surplus - addition
    return np.array(counts)


def scatter_about(key, dims, spread, reach, shards=(), kind=jnp.bfloat16):
    entries = spread * jax.random.normal(key, dims, jnp.float32)
    if shards:
        entries = entries * block_scale(key, dims, shards, -0.22, 0.18)
    return jnp.clip(entries, -reach, reach).astype(kind)


def setup_inputs(seed: int = 0) -> dict:
    splits = jax.random.split(jax.random.key(seed), 7)
    template = scatter_about(splits[0], (NZ, NY, NX), 1.0, 6.0, ((0, 8), (1, 4)), jnp.float32)
    fixed_image = scatter_about(splits[1], (NZ, NY, NX), 1.0, 6.0, ((0, 8), (1, 4)), jnp.float32)
    velocity = scatter_about(splits[2], (3, NZ, NY, NX), 0.3, 2.0, ((1, 8), (2, 4)), jnp.float32)
    src_owner_keys = jax.random.split(jax.random.fold_in(splits[3], 1), (N_SLAB * N_PENCIL * NB) // NB)
    src_owner_turns = jax.random.permutation(jax.random.fold_in(splits[3], 3), (N_SLAB * N_PENCIL * NB) // NB)
    src_owner = jax.vmap(lambda own, number: deal_out(jax.random.fold_in(splits[3], 2), own, number, NB, N_SLAB, K, C, 2))(src_owner_keys, src_owner_turns).reshape((N_SLAB * N_PENCIL * NB, K))
    src_local = plant(jax.random.randint(splits[4], (N_SLAB * N_PENCIL * NB, K), 0, NB), jax.random.fold_in(splits[4], 1), 0, NB - 1).astype(jnp.int32)
    weights = jnp.clip(0.2 + 0.8 * jax.random.uniform(splits[5], (N_SLAB * N_PENCIL * NB, K), jnp.float32) ** block_scale(splits[5], (N_SLAB * N_PENCIL * NB, K), ((0, 32),), -0.2, 0.2), 0.2, 1.0)
    return dict(template=template, fixed_image=fixed_image, velocity=velocity, src_owner=src_owner, src_local=src_local, weights=weights)


smooth_weight = 0.1
time_step = 0.5


def to_bricks(field):
    blocks = field.reshape(N_SLAB, BZ // BZB, BZB, N_PENCIL, BY // BYB, BYB, NX // BXB, BXB)
    blocks = blocks.transpose(0, 3, 1, 4, 6, 2, 5, 7)
    return blocks.reshape(N_SLAB * N_PENCIL * NB, BRICK)


def from_bricks(blocks):
    field = blocks.reshape(N_SLAB, N_PENCIL, BZ // BZB, BY // BYB, NX // BXB, BZB, BYB, BXB)
    field = field.transpose(0, 2, 5, 1, 3, 6, 4, 7)
    return field.reshape(NZ, NY, NX)


def pad_all(stacked):
    return jnp.pad(stacked, ((0, 0), (1, 1), (1, 1), (1, 1)))


def central_diff(padded):
    grad_z = (padded[:, 2:, 1:-1, 1:-1] - padded[:, :-2, 1:-1, 1:-1]) * 0.5
    grad_y = (padded[:, 1:-1, 2:, 1:-1] - padded[:, 1:-1, :-2, 1:-1]) * 0.5
    grad_x = (padded[:, 1:-1, 1:-1, 2:] - padded[:, 1:-1, 1:-1, :-2]) * 0.5
    return grad_z, grad_y, grad_x


def neighbours(padded):
    total = padded[:, 2:, 1:-1, 1:-1] + padded[:, :-2, 1:-1, 1:-1]
    total = total + padded[:, 1:-1, 2:, 1:-1] + padded[:, 1:-1, :-2, 1:-1]
    return total + padded[:, 1:-1, 1:-1, 2:] + padded[:, 1:-1, 1:-1, :-2]


def reference(template, fixed_image, velocity, src_owner, src_local, weights):
    own_bricks = to_bricks(template)
    target = to_bricks(fixed_image)
    row_pencil = ((jnp.arange(N_SLAB * N_PENCIL * NB, dtype=jnp.int32) // NB) % N_PENCIL).astype(jnp.int32)
    source = ((src_owner * N_PENCIL + row_pencil[:, None]) * NB + src_local).astype(jnp.int32)
    fetched = own_bricks[source]
    deformed = jnp.sum(weights[:, :, None] * fetched, axis=1)
    mismatch = deformed - target
    partial_terms = weights[:, :, None] * mismatch[:, None, :]
    adjoint = jax.ops.segment_sum(partial_terms.reshape(-1, BRICK), source.reshape(-1), num_segments=N_SLAB * N_PENCIL * NB)
    multiplier = from_bricks(adjoint)
    grad_z, grad_y, grad_x = central_diff(pad_all(template[None]))
    slopes = jnp.concatenate([grad_z, grad_y, grad_x], 0)
    body_force = multiplier[None] * slopes
    laplace = 6.0 * velocity - neighbours(pad_all(velocity))
    force_z, force_y, force_x = central_diff(pad_all(body_force))
    advect = velocity[0:1] * force_z + velocity[1:2] * force_y + velocity[2:3] * force_x
    return smooth_weight * laplace + body_force - time_step * advect
```

```python
import functools

import jax
import jax.numpy as jnp
from jax import lax
from jax.experimental import pallas as pl
from jax.experimental.pallas import tpu as pltpu
from jax.sharding import PartitionSpec as P

EDGE = 32
LANES = 128
QUADS = LANES // EDGE
MESH = pl.DeviceIdType.MESH
LIMIT = 50 * 1024 * 1024

smooth_weight = 0.1
time_step = 0.5


def whole(memory_space=pltpu.VMEM):
    return pl.BlockSpec(memory_space=memory_space)


def params(**kw):
    return pltpu.CompilerParams(vmem_limit_bytes=LIMIT, **kw)


def slots_kernel(owner_ref, local_ref, weight_ref, ids_ref, brick_ref, slot_weight_ref, pos_ref, count_ref):
    readers, capacity = ids_ref.shape
    bricks, picks = owner_ref.shape

    def clear(i, carry):
        count_ref[i] = 0
        for c in range(capacity):
            ids_ref[i, c] = 0
            brick_ref[i, c] = 0
            slot_weight_ref[i, c] = 0.0
        return carry

    lax.fori_loop(0, readers, clear, 0)

    def place(g, carry):
        for k in range(picks):
            owner = owner_ref[g, k]
            slot = count_ref[owner]
            count_ref[owner] = slot + 1
            ids_ref[owner, slot] = local_ref[g, k]
            brick_ref[owner, slot] = g
            slot_weight_ref[owner, slot] = weight_ref[g, k]
            pos_ref[g, k] = owner * capacity + slot
        return carry

    lax.fori_loop(0, bricks, place, 0)


def brick_at(brick, x_bricks):
    y_at = pl.multiple_of((brick // x_bricks) * EDGE, EDGE)
    x_brick = brick % x_bricks
    x_at = pl.multiple_of((x_brick // QUADS) * LANES, LANES)
    return y_at, x_at, x_brick % QUADS


def rotate(cells, quads):
    return pltpu.roll(cells, ((quads + QUADS) % QUADS) * EDGE, 2)


def lane_quad(shape):
    return lax.broadcasted_iota(jnp.int32, shape, 2) // EDGE


STEP = 2


def pack(field_ref, brick_of, weight_of, out_ref, lead, capacity):
    depth = EDGE * capacity // QUADS
    x_bricks = field_ref.shape[2] // EDGE
    places = [brick_at(brick_of(s), x_bricks) for s in range(capacity)]
    scale = None if weight_of is None else [weight_of(s) for s in range(capacity)]
    quad = lane_quad((STEP, EDGE, LANES))

    def body(i, carry):
        z = i * STEP
        total = jnp.zeros((STEP, EDGE, LANES), jnp.float32)
        for q in range(QUADS):
            s, part = q % capacity, q // capacity
            y_at, x_at, x_quad = places[s]
            cells = field_ref[pl.ds(part * depth + z, STEP), pl.ds(y_at, EDGE), pl.ds(x_at, LANES)]
            cells = rotate(cells, q - x_quad)
            if scale is not None:
                cells = cells * scale[s]
            total = jnp.where(quad == q, cells, total)
        out_ref[lead, pl.ds(z, STEP)] = total
        return carry

    lax.fori_loop(0, depth // STEP, body, 0)


def gather_kernel(ids_ref, field_ref, out_ref):
    reader = pl.program_id(0)
    capacity = ids_ref.shape[1]
    pack(field_ref, lambda s: ids_ref[reader, s], None, out_ref, 0, capacity)


def terms_kernel(pos_ref, weight_ref, brick_ref, slot_weight_ref, fixed_ref, got_ref, out_ref, mismatch_ref):
    reader = pl.program_id(0)
    capacity = brick_ref.shape[1]
    picks = pos_ref.shape[1]
    depth = EDGE * capacity // QUADS
    z_cells, y_cells, x_cells = fixed_ref.shape
    x_bricks = x_cells // EDGE

    @pl.when(reader == 0)
    def _():
        quad = lane_quad((STEP, EDGE, LANES))
        for y_brick in range(y_cells // EDGE):
            for x_tile in range(x_cells // LANES):
                terms = []
                for j in range(QUADS):
                    g = y_brick * x_bricks + x_tile * QUADS + j
                    for k in range(picks):
                        pos = pos_ref[g, k]
                        mask = jnp.where(quad == j, weight_ref[g, k], 0.0)
                        terms.append((pos // capacity, pos % capacity, j, mask))
                rows = pl.ds(y_brick * EDGE, EDGE)
                lanes = pl.ds(x_tile * LANES, LANES)
                for part in range(QUADS // capacity):

                    def body(i, carry, terms=terms, part=part, rows=rows, lanes=lanes):
                        z = i * STEP
                        planes = pl.ds(part * depth + z, STEP)
                        total = -fixed_ref[planes, rows, lanes]
                        for owner, slot, j, mask in terms:
                            cells = got_ref[owner, pl.ds(z, STEP)]
                            total = total + mask * rotate(cells, j - slot - part * capacity)
                        mismatch_ref[planes, rows, lanes] = total
                        return carry

                    lax.fori_loop(0, depth // STEP, body, 0)

    pack(
        mismatch_ref, lambda s: brick_ref[reader, s], lambda s: slot_weight_ref[reader, s], out_ref, 0, capacity
    )


def next_x(plane):
    lane = lax.broadcasted_iota(jnp.int32, plane.shape, 1)
    last = plane.shape[1] - 1
    after = jnp.where(lane == last, 0.0, pltpu.roll(plane, last, 1))
    before = jnp.where(lane == 0, 0.0, pltpu.roll(plane, 1, 1))
    return before, after


def next_y(plane, low, high):
    row = lax.broadcasted_iota(jnp.int32, plane.shape, 0)
    last = plane.shape[0] - 1
    after = jnp.where(row == last, high, pltpu.roll(plane, last, 0))
    before = jnp.where(row == 0, low, pltpu.roll(plane, 1, 0))
    return before, after


def adjoint_kernel(ids_ref, got_ref, field_ref, z_low_ref, z_high_ref, y_low_ref, y_high_ref, force_ref, sum_ref):
    readers, capacity = ids_ref.shape
    depth = EDGE * capacity // QUADS
    z_cells, y_cells, x_cells = field_ref.shape
    x_bricks = x_cells // EDGE
    quad = lane_quad((STEP, EDGE, LANES))
    sum_ref[...] = jnp.zeros_like(sum_ref)

    def add(reader, carry):
        for s in range(capacity):
            y_at, x_at, x_quad = brick_at(ids_ref[reader, s], x_bricks)
            for part in range(QUADS // capacity):

                def body(i, inner, s=s, part=part, y_at=y_at, x_at=x_at, x_quad=x_quad):
                    z = i * STEP
                    cells = rotate(got_ref[reader, pl.ds(z, STEP)], x_quad - s - part * capacity)
                    place = (pl.ds(part * depth + z, STEP), pl.ds(y_at, EDGE), pl.ds(x_at, LANES))
                    sum_ref[place] = sum_ref[place] + jnp.where(quad == x_quad, cells, 0.0)
                    return inner

                lax.fori_loop(0, depth // STEP, body, 0, unroll=2)
        return carry

    lax.fori_loop(0, readers, add, 0)

    def plane(z, carry):
        here = field_ref[z]
        below = jnp.where(z == 0, z_low_ref[0], field_ref[jnp.maximum(z - 1, 0)])
        above = jnp.where(z == z_cells - 1, z_high_ref[0], field_ref[jnp.minimum(z + 1, z_cells - 1)])
        half = 0.5 * sum_ref[z]
        before_y, after_y = next_y(here, y_low_ref[pl.ds(z, 1)], y_high_ref[pl.ds(z, 1)])
        before_x, after_x = next_x(here)
        force_ref[0, z] = half * (above - below)
        force_ref[1, z] = half * (after_y - before_y)
        force_ref[2, z] = half * (after_x - before_x)
        return carry

    lax.fori_loop(0, z_cells, plane, 0)


def gradient_kernel(
    vel_ref, vel_before_ref, vel_after_ref, vz_low_ref, vz_high_ref, vy_low_ref, vy_high_ref,
    frc_ref, frc_before_ref, frc_after_ref, fz_low_ref, fz_high_ref, fy_low_ref, fy_high_ref, out_ref,
):
    block = pl.program_id(0)
    blocks = pl.num_programs(0)
    planes = vel_ref.shape[1]

    def around(ref, before_ref, after_ref, low_ref, high_ref, y_low_ref, y_high_ref, c, z):
        here = ref[c, z]
        if z == 0:
            below = jnp.where(block == 0, low_ref[c], before_ref[c, 0])
        else:
            below = ref[c, z - 1]
        if z == planes - 1:
            above = jnp.where(block == blocks - 1, high_ref[c], after_ref[c, 0])
        else:
            above = ref[c, z + 1]
        before_y, after_y = next_y(here, y_low_ref[c, z:z + 1], y_high_ref[c, z:z + 1])
        before_x, after_x = next_x(here)
        return here, below, above, before_y, after_y, before_x, after_x

    for z in range(planes):
        half = [0.5 * time_step * vel_ref[i, z] for i in range(3)]
        for c in range(3):
            v = around(vel_ref, vel_before_ref, vel_after_ref, vz_low_ref, vz_high_ref, vy_low_ref, vy_high_ref, c, z)
            laplace = 6.0 * v[0] - (((v[1] + v[2]) + (v[3] + v[4])) + (v[5] + v[6]))
            f = around(frc_ref, frc_before_ref, frc_after_ref, fz_low_ref, fz_high_ref, fy_low_ref, fy_high_ref, c, z)
            advect = half[0] * (f[2] - f[1]) + half[1] * (f[4] - f[3]) + half[2] * (f[6] - f[5])
            out_ref[c, z] = smooth_weight * laplace + f[0] - advect


def partner(me, offset, count):
    other, bit = 0, 1
    while bit < count:
        other = other + ((me // bit + (offset // bit) % 2) % 2) * bit
        bit = bit * 2
    return other


def exchange_kernel(count, src_ref, dst_ref, send_sem, recv_sem, own_sem):
    me = lax.axis_index("slab")
    order = sorted(range(1, count), key=lambda j: -bin(j // 2).count("1"))
    barrier = pltpu.get_barrier_semaphore()
    for j in order:
        pl.semaphore_signal(barrier, inc=1, device_id={"slab": partner(me, j, count)}, device_id_type=MESH)
    own = pltpu.make_async_copy(src_ref.at[me], dst_ref.at[me], own_sem)
    own.start()
    pl.semaphore_wait(barrier, count - 1)
    copies = []
    for j in order:
        other = partner(me, j, count)
        copy = pltpu.make_async_remote_copy(
            src_ref=src_ref.at[other],
            dst_ref=dst_ref.at[me],
            send_sem=send_sem.at[j],
            recv_sem=recv_sem.at[j],
            device_id={"slab": other},
            device_id_type=MESH,
        )
        copy.start()
        copies.append(copy)
    own.wait()
    for copy in copies:
        copy.wait()


def exchange(blocks, count, collective_id):
    return pl.pallas_call(
        functools.partial(exchange_kernel, count),
        out_shape=jax.ShapeDtypeStruct(blocks.shape, blocks.dtype),
        in_specs=[whole(pl.ANY)],
        out_specs=whole(pl.ANY),
        scratch_shapes=[
            pltpu.SemaphoreType.DMA((count,)),
            pltpu.SemaphoreType.DMA((count,)),
            pltpu.SemaphoreType.DMA,
        ],
        compiler_params=pltpu.CompilerParams(collective_id=collective_id, has_side_effects=True),
        name="exchange%d" % collective_id,
    )(blocks)


def faces(cells, axis, dim):
    count = lax.axis_size(axis)
    size = cells.shape[dim]
    tail = lax.slice_in_dim(cells, size - 1, size, axis=dim)
    head = lax.slice_in_dim(cells, 0, 1, axis=dim)
    if dim == cells.ndim - 2:
        tail, head = jnp.squeeze(tail, dim), jnp.squeeze(head, dim)
    low = lax.ppermute(tail, axis, [(i, i + 1) for i in range(count - 1)])
    high = lax.ppermute(head, axis, [(i + 1, i) for i in range(count - 1)])
    return low, high


def per_device(template, fixed_image, velocity, src_owner, src_local, weights):
    slab_count = lax.axis_size("slab")
    bricks, picks = src_owner.shape
    capacity = max(2, bricks * picks // slab_count)
    z_cells, y_cells, x_cells = template.shape
    depth = EDGE * capacity // QUADS
    f32, i32 = jnp.float32, jnp.int32
    smem = whole(pltpu.SMEM)
    table = (slab_count, capacity)

    ids, brick_of, slot_weight, pos = pl.pallas_call(
        slots_kernel,
        out_shape=(
            jax.ShapeDtypeStruct(table, i32),
            jax.ShapeDtypeStruct(table, i32),
            jax.ShapeDtypeStruct(table, f32),
            jax.ShapeDtypeStruct((bricks, picks), i32),
        ),
        in_specs=[smem] * 3,
        out_specs=(smem,) * 4,
        scratch_shapes=[pltpu.SMEM((slab_count,), i32)],
        name="slots",
    )(src_owner, src_local, weights)
    requested = lax.all_to_all(ids, "slab", split_axis=0, concat_axis=0, tiled=True)

    fields = jnp.concatenate([template[None], velocity], 0)
    z_low, z_high = faces(fields, "slab", 1)
    y_low, y_high = faces(fields, "pencil", 2)

    packed = (slab_count, depth, EDGE, LANES)
    packed_spec = pl.BlockSpec((1, depth, EDGE, LANES), lambda d: (d, 0, 0, 0))
    outgoing = pl.pallas_call(
        gather_kernel,
        grid=(slab_count,),
        out_shape=jax.ShapeDtypeStruct(packed, f32),
        in_specs=[smem, whole()],
        out_specs=packed_spec,
        compiler_params=params(),
        name="gather",
    )(requested, template)
    fetched = exchange(outgoing, slab_count, 1)
    terms = pl.pallas_call(
        terms_kernel,
        grid=(slab_count,),
        out_shape=jax.ShapeDtypeStruct(packed, f32),
        in_specs=[smem] * 4 + [whole()] * 2,
        out_specs=packed_spec,
        scratch_shapes=[pltpu.VMEM(template.shape, f32)],
        compiler_params=params(),
        name="terms",
    )(pos, weights, brick_of, slot_weight, fixed_image, fetched)
    returned = exchange(terms, slab_count, 2)
    force = pl.pallas_call(
        adjoint_kernel,
        out_shape=jax.ShapeDtypeStruct((3,) + template.shape, f32),
        in_specs=[smem] + [whole()] * 6,
        out_specs=whole(),
        scratch_shapes=[pltpu.VMEM(template.shape, f32)],
        compiler_params=params(),
        name="adjoint",
    )(requested, returned, template, z_low[0], z_high[0], y_low[0], y_high[0])

    fz_low, fz_high = faces(force, "slab", 1)
    fy_low, fy_high = faces(force, "pencil", 2)
    rows = 8
    last = z_cells - 1
    block = (3, rows, y_cells, x_cells)
    plane = (3, 1, y_cells, x_cells)
    field_specs = [
        pl.BlockSpec(block, lambda z: (0, z, 0, 0)),
        pl.BlockSpec(plane, lambda z: (0, jnp.maximum(z * rows - 1, 0), 0, 0)),
        pl.BlockSpec(plane, lambda z: (0, jnp.minimum(z * rows + rows, last), 0, 0)),
        pl.BlockSpec((3, y_cells, x_cells), lambda z: (0, 0, 0)),
        pl.BlockSpec((3, y_cells, x_cells), lambda z: (0, 0, 0)),
        pl.BlockSpec((3, rows, x_cells), lambda z: (0, z, 0)),
        pl.BlockSpec((3, rows, x_cells), lambda z: (0, z, 0)),
    ]
    return pl.pallas_call(
        gradient_kernel,
        grid=(z_cells // rows,),
        out_shape=jax.ShapeDtypeStruct(velocity.shape, f32),
        in_specs=field_specs + field_specs,
        out_specs=pl.BlockSpec(block, lambda z: (0, z, 0, 0)),
        compiler_params=params(),
        name="gradient",
    )(
        velocity, velocity, velocity, z_low[1:, 0], z_high[1:, 0], y_low[1:], y_high[1:],
        force, force, force, fz_low[:, 0], fz_high[:, 0], fy_low, fy_high,
    )


def solution(mesh):
    in_specs = (
        P("slab", "pencil", None),
        P("slab", "pencil", None),
        P(None, "slab", "pencil", None),
        P(("slab", "pencil"), None),
        P(("slab", "pencil"), None),
        P(("slab", "pencil"), None),
    )
    out_specs = P(None, "slab", "pencil", None)
    return jax.shard_map(
        per_device, mesh=mesh, in_specs=in_specs, out_specs=out_specs, check_vma=False
    )
```

```python
import functools

import jax
import jax.numpy as jnp
from jax import lax
from jax.experimental import pallas as pl
from jax.experimental.pallas import tpu as pltpu
from jax.sharding import PartitionSpec as P

EDGE = 32
LANES = 128
QUADS = LANES // EDGE
MESH = pl.DeviceIdType.MESH
LIMIT = 50 * 1024 * 1024

smooth_weight = 0.1
time_step = 0.5


def whole(memory_space=pltpu.VMEM):
    return pl.BlockSpec(memory_space=memory_space)


def params(**kw):
    return pltpu.CompilerParams(vmem_limit_bytes=LIMIT, **kw)


def slots_kernel(owner_ref, local_ref, weight_ref, ids_ref, brick_ref, slot_weight_ref, count_ref):
    readers, capacity = ids_ref.shape
    bricks, picks = owner_ref.shape

    def clear(i, carry):
        count_ref[i] = 0
        for c in range(capacity):
            ids_ref[i, c] = 0
            brick_ref[i, c] = 0
            slot_weight_ref[i, c] = 0.0
        return carry

    lax.fori_loop(0, readers, clear, 0)

    def place(g, carry):
        for k in range(picks):
            owner = owner_ref[g, k]
            slot = count_ref[owner]
            count_ref[owner] = slot + 1
            ids_ref[owner, slot] = local_ref[g, k]
            brick_ref[owner, slot] = g
            slot_weight_ref[owner, slot] = weight_ref[g, k]
        return carry

    lax.fori_loop(0, bricks, place, 0)


def masks_of(brick_ref, weight_ref, lead, sign, part, tile_count):
    capacity = brick_ref.shape[1]
    quad = lax.broadcasted_iota(jnp.int32, (8, LANES), 1) // EDGE
    masks = [[] for _ in range(tile_count)]
    for r in range(QUADS):
        brick = jnp.full((8, LANES), -1, jnp.int32)
        weight = jnp.ones((8, LANES), jnp.float32)
        for j in range(QUADS):
            q = (j - sign * r) % QUADS
            if q // capacity == part:
                brick = jnp.where(quad == j, brick_ref[lead, q % capacity], brick)
                if weight_ref is not None:
                    weight = jnp.where(quad == j, weight_ref[lead, q % capacity], weight)
        for t in range(tile_count):
            masks[t].append(jnp.where(brick == t * QUADS + quad, weight, 0.0)[None])
    return masks


def tiles_of(field_ref):
    x_tiles = field_ref.shape[2] // LANES
    return [(y, x) for y in range(field_ref.shape[1] // EDGE) for x in range(x_tiles)]


STEP = 4
ROWS = STEP * EDGE // 8


def pack(field_ref, brick_ref, weight_ref, lead, out_ref):
    capacity = brick_ref.shape[1]
    depth = EDGE * capacity // QUADS
    parts = range(QUADS // capacity)
    tiles = tiles_of(field_ref)
    masks = [masks_of(brick_ref, weight_ref, lead, -1, part, len(tiles)) for part in parts]

    def body(i, carry):
        z = i * STEP
        sums = [None] * QUADS
        for part in parts:
            for t, (y, x) in enumerate(tiles):
                cells = field_ref[pl.ds(part * depth + z, STEP), pl.ds(y * EDGE, EDGE), pl.ds(x * LANES, LANES)]
                cells = cells.reshape(ROWS, 8, LANES)
                for r in range(QUADS):
                    term = masks[part][t][r] * cells
                    sums[r] = term if sums[r] is None else sums[r] + term
        total = sums[0]
        for r in range(1, QUADS):
            total = total + pltpu.roll(sums[r], r * EDGE, 2)
        out_ref[lead, pl.ds(z, STEP)] = total.reshape(STEP, EDGE, LANES)
        return carry

    lax.fori_loop(0, depth // STEP, body, 0)


def accumulate(got_ref, brick_ref, weight_ref, lead, sum_ref):
    capacity = brick_ref.shape[1]
    depth = EDGE * capacity // QUADS
    parts = range(QUADS // capacity)
    tiles = tiles_of(sum_ref)
    masks = [masks_of(brick_ref, weight_ref, lead, 1, part, len(tiles)) for part in parts]

    def body(i, carry):
        z = i * STEP
        cells = got_ref[lead, pl.ds(z, STEP)].reshape(ROWS, 8, LANES)
        turned = [cells] + [pltpu.roll(cells, r * EDGE, 2) for r in range(1, QUADS)]
        for part in parts:
            for t, (y, x) in enumerate(tiles):
                total = masks[part][t][0] * turned[0]
                for r in range(1, QUADS):
                    total = total + masks[part][t][r] * turned[r]
                at = (pl.ds(part * depth + z, STEP), pl.ds(y * EDGE, EDGE), pl.ds(x * LANES, LANES))
                sum_ref[at] = sum_ref[at] + total.reshape(STEP, EDGE, LANES)
        return carry

    lax.fori_loop(0, depth // STEP, body, 0)


def next_x(plane):
    lane = lax.broadcasted_iota(jnp.int32, plane.shape, 1)
    last = plane.shape[1] - 1
    after = jnp.where(lane == last, 0.0, pltpu.roll(plane, last, 1))
    before = jnp.where(lane == 0, 0.0, pltpu.roll(plane, 1, 1))
    return before, after


def next_y(plane, low, high):
    row = lax.broadcasted_iota(jnp.int32, plane.shape, 0)
    last = plane.shape[0] - 1
    after = jnp.where(row == last, high, pltpu.roll(plane, last, 0))
    before = jnp.where(row == 0, low, pltpu.roll(plane, 1, 0))
    return before, after


def partner(me, offset, count):
    other, bit = 0, 1
    while bit < count:
        other = other + ((me // bit + (offset // bit) % 2) % 2) * bit
        bit = bit * 2
    return other


def ring(axis):
    me, count = lax.axis_index(axis), lax.axis_size(axis)
    return (me + count - 1) % count, (me + 1) % count


def meet(count):
    barrier = pltpu.get_barrier_semaphore()
    me = lax.axis_index("slab")

    def greet(j, carry):
        other = partner(me, j, count)
        pl.semaphore_signal(barrier, inc=1, device_id={"slab": other}, device_id_type=MESH)
        return carry

    lax.fori_loop(1, count, greet, 0)
    for other in ring("pencil"):
        pl.semaphore_signal(barrier, inc=1, device_id={"pencil": other}, device_id_type=MESH)
    pl.semaphore_wait(barrier, count - 1 + 2)


def send(src, dst, sems, i, axis, other):
    return pltpu.make_async_remote_copy(
        src_ref=src, dst_ref=dst, send_sem=sems.at[0, i], recv_sem=sems.at[1, i],
        device_id={axis: other}, device_id_type=MESH,
    )


def swap(count, out_ref, got_ref, sems, fill, take):
    me = lax.axis_index("slab")

    def copy(j):
        other = partner(me, j, count)
        return other, send(out_ref.at[other], got_ref.at[me], sems, j, "slab", other)

    def start(i, carry):
        other, block = copy(count - 1 - i)
        fill(other)
        block.start()
        return carry

    lax.fori_loop(0, count - 1, start, 0)
    fill(me)
    take(out_ref, me)

    def finish(j, carry):
        other, block = copy(j)
        block.wait_recv()
        take(got_ref, other)
        return carry

    lax.fori_loop(1, count, finish, 0)

    def drain(j, carry):
        copy(j)[1].wait_send()
        return carry

    lax.fori_loop(1, count, drain, 0)


def forward_kernel(
    count, ids_ref, brick_ref, weight_ref, tpl_ref, fixed_ref, vel_ref,
    miss_ref, tz_low, tz_high, vz_low, vz_high, ty_low, ty_high, vy_low, vy_high,
    out_ref, got_ref, sems, halo_sems,
):
    z_cells, y_cells, _ = tpl_ref.shape
    meet(count)
    below, above = ring("slab")
    left, right = ring("pencil")
    z_last, y_last = pl.ds(z_cells - 1, 1), pl.ds(y_cells - 8, 8)
    z_head, y_head = pl.ds(0, 1), pl.ds(0, 8)
    halos = [
        send(tpl_ref.at[z_last], tz_low, halo_sems, 0, "slab", above),
        send(tpl_ref.at[z_head], tz_high, halo_sems, 1, "slab", below),
        send(vel_ref.at[:, z_last], vz_low, halo_sems, 2, "slab", above),
        send(vel_ref.at[:, z_head], vz_high, halo_sems, 3, "slab", below),
        send(tpl_ref.at[:, y_last], ty_low, halo_sems, 4, "pencil", right),
        send(tpl_ref.at[:, y_head], ty_high, halo_sems, 5, "pencil", left),
        send(vel_ref.at[:, :, y_last], vy_low, halo_sems, 6, "pencil", right),
        send(vel_ref.at[:, :, y_head], vy_high, halo_sems, 7, "pencil", left),
    ]
    for halo in halos:
        halo.start()
    miss_ref[...] = -fixed_ref[...]
    swap(
        count, out_ref, got_ref, sems,
        lambda other: pack(tpl_ref, ids_ref, None, other, out_ref),
        lambda ref, other: accumulate(ref, brick_ref, weight_ref, other, miss_ref),
    )
    for halo in halos:
        halo.wait()


def backward_kernel(
    count, ids_ref, brick_ref, weight_ref, miss_ref, tpl_ref, tz_low, tz_high, ty_low, ty_high,
    force_ref, fz_low, fz_high, fy_low, fy_high,
    out_ref, got_ref, sum_ref, head_ref, tail_ref, sems, halo_sems,
):
    z_cells, y_cells, _ = tpl_ref.shape
    meet(count)
    sum_ref[...] = jnp.zeros_like(sum_ref)
    swap(
        count, out_ref, got_ref, sems,
        lambda other: pack(miss_ref, brick_ref, weight_ref, other, out_ref),
        lambda ref, other: accumulate(ref, ids_ref, None, other, sum_ref),
    )
    slab, pencil = lax.axis_index("slab"), lax.axis_index("pencil")
    keep_below = jnp.where(slab == 0, 0.0, 1.0)
    keep_above = jnp.where(slab == count - 1, 0.0, 1.0)
    keep_left = jnp.where(pencil == 0, 0.0, 1.0)
    keep_right = jnp.where(pencil == lax.axis_size("pencil") - 1, 0.0, 1.0)

    def plane(z, below, above):
        here = tpl_ref[z]
        half = 0.5 * sum_ref[z]
        before_y, after_y = next_y(here, keep_left * ty_low[z, 7:8], keep_right * ty_high[z, 0:1])
        before_x, after_x = next_x(here)
        for c, slope in enumerate((above - below, after_y - before_y, after_x - before_x)):
            force = half * slope
            force_ref[c, z] = force
            head_ref[c, pl.ds(z, 1)] = force[0:1]
            tail_ref[c, pl.ds(z, 1)] = force[y_cells - 1:y_cells]

    plane(0, keep_below * tz_low[0], tpl_ref[1])
    plane(z_cells - 1, tpl_ref[z_cells - 2], keep_above * tz_high[0])
    below, above = ring("slab")
    left, right = ring("pencil")
    halos = [
        send(force_ref.at[:, pl.ds(z_cells - 1, 1)], fz_low, halo_sems, 0, "slab", above),
        send(force_ref.at[:, pl.ds(0, 1)], fz_high, halo_sems, 1, "slab", below),
        send(tail_ref, fy_low, halo_sems, 2, "pencil", right),
        send(head_ref, fy_high, halo_sems, 3, "pencil", left),
    ]
    halos[0].start()
    halos[1].start()

    def inner(z, carry):
        plane(z, tpl_ref[z - 1], tpl_ref[z + 1])
        return carry

    lax.fori_loop(1, z_cells - 1, inner, 0)
    halos[2].start()
    halos[3].start()
    for halo in halos:
        halo.wait()


def gradient_kernel(
    vel_ref, vel_before_ref, vel_after_ref, vz_low_ref, vz_high_ref, vy_low_ref, vy_high_ref,
    frc_ref, frc_before_ref, frc_after_ref, fz_low_ref, fz_high_ref, fy_low_ref, fy_high_ref, out_ref,
):
    block = pl.program_id(0)
    blocks = pl.num_programs(0)
    planes = vel_ref.shape[1]

    slab, pencil = lax.axis_index("slab"), lax.axis_index("pencil")
    keep_below = jnp.where(slab == 0, 0.0, 1.0)
    keep_above = jnp.where(slab == lax.axis_size("slab") - 1, 0.0, 1.0)
    keep_left = jnp.where(pencil == 0, 0.0, 1.0)
    keep_right = jnp.where(pencil == lax.axis_size("pencil") - 1, 0.0, 1.0)

    def around(ref, before_ref, after_ref, low_ref, high_ref, y_low, y_high, c, z):
        here = ref[c, z]
        if z == 0:
            below = jnp.where(block == 0, keep_below * low_ref[c, 0], before_ref[c, 0])
        else:
            below = ref[c, z - 1]
        if z == planes - 1:
            above = jnp.where(block == blocks - 1, keep_above * high_ref[c, 0], after_ref[c, 0])
        else:
            above = ref[c, z + 1]
        before_y, after_y = next_y(here, keep_left * y_low, keep_right * y_high)
        before_x, after_x = next_x(here)
        return here, below, above, before_y, after_y, before_x, after_x

    for z in range(planes):
        half = [0.5 * time_step * vel_ref[i, z] for i in range(3)]
        for c in range(3):
            v = around(vel_ref, vel_before_ref, vel_after_ref, vz_low_ref, vz_high_ref, vy_low_ref[c, z, 7:8], vy_high_ref[c, z, 0:1], c, z)
            laplace = 6.0 * v[0] - (((v[1] + v[2]) + (v[3] + v[4])) + (v[5] + v[6]))
            f = around(frc_ref, frc_before_ref, frc_after_ref, fz_low_ref, fz_high_ref, fy_low_ref[c, z:z + 1], fy_high_ref[c, z:z + 1], c, z)
            advect = half[0] * (f[2] - f[1]) + half[1] * (f[4] - f[3]) + half[2] * (f[6] - f[5])
            out_ref[c, z] = smooth_weight * laplace + f[0] - advect


def per_device(template, fixed_image, velocity, src_owner, src_local, weights):
    slab_count = lax.axis_size("slab")
    bricks, picks = src_owner.shape
    capacity = max(2, bricks * picks // slab_count)
    z_cells, y_cells, x_cells = template.shape
    depth = EDGE * capacity // QUADS
    f32, i32 = jnp.float32, jnp.int32
    smem = whole(pltpu.SMEM)
    table = (slab_count, capacity)

    ids, brick_of, slot_weight = pl.pallas_call(
        slots_kernel,
        out_shape=(
            jax.ShapeDtypeStruct(table, i32),
            jax.ShapeDtypeStruct(table, i32),
            jax.ShapeDtypeStruct(table, f32),
        ),
        in_specs=[smem] * 3,
        out_specs=(smem,) * 3,
        scratch_shapes=[pltpu.SMEM((slab_count,), i32)],
        name="slots",
    )(src_owner, src_local, weights)
    requested = lax.all_to_all(ids, "slab", split_axis=0, concat_axis=0, tiled=True)

    packed = (slab_count, depth, EDGE, LANES)
    z_face, y_face = (1, y_cells, x_cells), (z_cells, 8, x_cells)
    shapes = [template.shape, z_face, z_face, (3,) + z_face, (3,) + z_face]
    shapes += [y_face, y_face, (3,) + y_face, (3,) + y_face]
    sems = [pltpu.SemaphoreType.DMA((2, slab_count)), pltpu.SemaphoreType.DMA((2, 8))]
    miss, tz_low, tz_high, vz_low, vz_high, ty_low, ty_high, vy_low, vy_high = pl.pallas_call(
        functools.partial(forward_kernel, slab_count),
        out_shape=[jax.ShapeDtypeStruct(shape, f32) for shape in shapes],
        in_specs=[smem] * 3 + [whole(), whole(), whole(pl.ANY)],
        out_specs=[whole()] + [whole(pl.ANY)] * 8,
        scratch_shapes=[pltpu.VMEM(packed, f32), pltpu.VMEM(packed, f32)] + sems,
        compiler_params=params(collective_id=1, has_side_effects=True),
        name="forward",
    )(requested, brick_of, slot_weight, template, fixed_image, velocity)

    shapes = [(3,) + template.shape, (3,) + z_face, (3,) + z_face, (3, z_cells, x_cells), (3, z_cells, x_cells)]
    edge = pltpu.VMEM((3, z_cells, x_cells), f32)
    force, fz_low, fz_high, fy_low, fy_high = pl.pallas_call(
        functools.partial(backward_kernel, slab_count),
        out_shape=[jax.ShapeDtypeStruct(shape, f32) for shape in shapes],
        in_specs=[smem] * 3 + [whole()] * 6,
        out_specs=[whole()] + [whole(pl.ANY)] * 4,
        scratch_shapes=[pltpu.VMEM(packed, f32), pltpu.VMEM(packed, f32), pltpu.VMEM(template.shape, f32), edge, edge] + sems,
        compiler_params=params(collective_id=2, has_side_effects=True),
        name="backward",
    )(requested, brick_of, slot_weight, miss, template, tz_low, tz_high, ty_low, ty_high)

    rows = 8
    last = z_cells - 1
    block = (3, rows, y_cells, x_cells)
    plane = (3, 1, y_cells, x_cells)
    z_spec = pl.BlockSpec(plane, lambda z: (0, 0, 0, 0))
    field_specs = [
        pl.BlockSpec(block, lambda z: (0, z, 0, 0)),
        pl.BlockSpec(plane, lambda z: (0, jnp.maximum(z * rows - 1, 0), 0, 0)),
        pl.BlockSpec(plane, lambda z: (0, jnp.minimum(z * rows + rows, last), 0, 0)),
        z_spec,
        z_spec,
    ]
    vy_spec = pl.BlockSpec((3, rows, 8, x_cells), lambda z: (0, z, 0, 0))
    fy_spec = pl.BlockSpec((3, rows, x_cells), lambda z: (0, z, 0))
    return pl.pallas_call(
        gradient_kernel,
        grid=(z_cells // rows,),
        out_shape=jax.ShapeDtypeStruct(velocity.shape, f32),
        in_specs=field_specs + [vy_spec] * 2 + field_specs + [fy_spec] * 2,
        out_specs=pl.BlockSpec(block, lambda z: (0, z, 0, 0)),
        compiler_params=params(),
        name="gradient",
    )(
        velocity, velocity, velocity, vz_low, vz_high, vy_low, vy_high,
        force, force, force, fz_low, fz_high, fy_low, fy_high,
    )


def solution(mesh):
    in_specs = (
        P("slab", "pencil", None),
        P("slab", "pencil", None),
        P(None, "slab", "pencil", None),
        P(("slab", "pencil"), None),
        P(("slab", "pencil"), None),
        P(("slab", "pencil"), None),
    )
    out_specs = P(None, "slab", "pencil", None)
    return jax.shard_map(
        per_device, mesh=mesh, in_specs=in_specs, out_specs=out_specs, check_vma=False
    )
```

```python
import functools

import jax
import jax.numpy as jnp
from jax import lax
from jax.experimental import pallas as pl
from jax.experimental.pallas import tpu as pltpu
from jax.sharding import PartitionSpec as P

EDGE = 32
LANES = 128
QUADS = LANES // EDGE
MESH = pl.DeviceIdType.MESH
LIMIT = 56 * 1024 * 1024
CHUNKS = 4

smooth_weight = 0.1
time_step = 0.5


def whole(memory_space=pltpu.VMEM):
    return pl.BlockSpec(memory_space=memory_space)


def params(**kw):
    return pltpu.CompilerParams(vmem_limit_bytes=LIMIT, **kw)


def lane_quad():
    return lax.broadcasted_iota(jnp.int32, (8, LANES), 1) // EDGE


def slots_kernel(
    owner_ref, local_ref, weight_ref, ids_out, brick_out, weight_out, ids_ref, brick_ref, slot_weight_ref, count_ref
):
    readers, capacity = ids_ref.shape
    bricks, picks = owner_ref.shape

    def clear(i, carry):
        count_ref[i] = 0
        for c in range(capacity):
            ids_ref[i, c] = 0
            brick_ref[i, c] = 0
            slot_weight_ref[i, c] = 0.0
        return carry

    lax.fori_loop(0, readers, clear, 0)

    def place(g, carry):
        for k in range(picks):
            owner = owner_ref[g, k]
            slot = count_ref[owner]
            count_ref[owner] = slot + 1
            ids_ref[owner, slot] = local_ref[g, k]
            brick_ref[owner, slot] = g
            slot_weight_ref[owner, slot] = weight_ref[g, k]
        return carry

    lax.fori_loop(0, bricks, place, 0)
    quad = lane_quad()

    def spread(i, carry):
        for ref, out in ((ids_ref, ids_out), (brick_ref, brick_out), (slot_weight_ref, weight_out)):
            row = jnp.full((8, LANES), ref[i, 0])
            for q in range(1, QUADS):
                row = jnp.where(quad == q, ref[i, q % capacity], row)
            out[i] = row
        return carry

    lax.fori_loop(0, readers, spread, 0)


def masks_of(brick_ref, weight_ref, lead, sign, part, capacity, tile_count):
    quad = lane_quad()
    brick, weight = brick_ref[lead], jnp.ones((8, LANES), jnp.float32)
    if weight_ref is not None:
        weight = weight_ref[lead]
    masks = [[] for _ in range(tile_count)]
    for r in range(QUADS):
        turn = (sign * r % QUADS) * EDGE
        here = pltpu.roll(brick, turn, 1) if turn else brick
        scale = pltpu.roll(weight, turn, 1) if turn and weight_ref is not None else weight
        if capacity < QUADS:
            here = jnp.where((quad - sign * r + QUADS) % QUADS // capacity == part, here, -1)
        for t in range(tile_count):
            masks[t].append(jnp.where(here == t * QUADS + quad, scale, 0.0)[None])
    return masks


def tiles_of(field_ref):
    x_tiles = field_ref.shape[2] // LANES
    return [(y, x) for y in range(field_ref.shape[1] // EDGE) for x in range(x_tiles)]


STEP = 4
ROWS = STEP * EDGE // 8


def pack(field_ref, brick_ref, weight_ref, lead, chunk, out_ref):
    depth = out_ref.shape[1]
    capacity = QUADS * depth // EDGE
    parts = range(QUADS // capacity)
    size = depth // CHUNKS
    tiles = tiles_of(field_ref)
    masks = [masks_of(brick_ref, weight_ref, lead, -1, part, capacity, len(tiles)) for part in parts]

    def body(i, carry):
        z = chunk * size + i * STEP
        sums = [None] * QUADS
        for part in parts:
            for t, (y, x) in enumerate(tiles):
                cells = field_ref[pl.ds(part * depth + z, STEP), pl.ds(y * EDGE, EDGE), pl.ds(x * LANES, LANES)]
                cells = cells.reshape(ROWS, 8, LANES)
                for r in range(QUADS):
                    term = masks[part][t][r] * cells
                    sums[r] = term if sums[r] is None else sums[r] + term
        total = sums[0]
        for r in range(1, QUADS):
            total = total + pltpu.roll(sums[r], r * EDGE, 2)
        out_ref[lead, pl.ds(z, STEP)] = total.reshape(STEP, EDGE, LANES)
        return carry

    lax.fori_loop(0, size // STEP, body, 0)


def accumulate(got_ref, brick_ref, weight_ref, lead, chunk, sum_ref):
    depth = got_ref.shape[1]
    capacity = QUADS * depth // EDGE
    parts = range(QUADS // capacity)
    size = depth // CHUNKS
    tiles = tiles_of(sum_ref)
    masks = [masks_of(brick_ref, weight_ref, lead, 1, part, capacity, len(tiles)) for part in parts]

    def body(i, carry):
        z = chunk * size + i * STEP
        cells = got_ref[lead, pl.ds(z, STEP)].reshape(ROWS, 8, LANES)
        turned = [cells] + [pltpu.roll(cells, r * EDGE, 2) for r in range(1, QUADS)]
        for part in parts:
            for t, (y, x) in enumerate(tiles):
                total = masks[part][t][0] * turned[0]
                for r in range(1, QUADS):
                    total = total + masks[part][t][r] * turned[r]
                at = (pl.ds(part * depth + z, STEP), pl.ds(y * EDGE, EDGE), pl.ds(x * LANES, LANES))
                sum_ref[at] = sum_ref[at] + total.reshape(STEP, EDGE, LANES)
        return carry

    lax.fori_loop(0, size // STEP, body, 0)


def next_x(plane):
    lane = lax.broadcasted_iota(jnp.int32, plane.shape, 1)
    last = plane.shape[1] - 1
    after = jnp.where(lane == last, 0.0, pltpu.roll(plane, last, 1))
    before = jnp.where(lane == 0, 0.0, pltpu.roll(plane, 1, 1))
    return before, after


def next_y(plane, low, high):
    row = lax.broadcasted_iota(jnp.int32, plane.shape, 0)
    last = plane.shape[0] - 1
    after = jnp.where(row == last, high, pltpu.roll(plane, last, 0))
    before = jnp.where(row == 0, low, pltpu.roll(plane, 1, 0))
    return before, after


def partner(me, offset, count):
    other, bit = 0, 1
    while bit < count:
        other = other + ((me // bit + (offset // bit) % 2) % 2) * bit
        bit = bit * 2
    return other


def ring(axis):
    me, count = lax.axis_index(axis), lax.axis_size(axis)
    return (me + count - 1) % count, (me + 1) % count


def meet(count):
    barrier = pltpu.get_barrier_semaphore()
    me = lax.axis_index("slab")

    def greet(j, carry):
        other = partner(me, j, count)
        pl.semaphore_signal(barrier, inc=1, device_id={"slab": other}, device_id_type=MESH)
        return carry

    lax.fori_loop(1, count, greet, 0)
    for other in ring("pencil"):
        pl.semaphore_signal(barrier, inc=1, device_id={"pencil": other}, device_id_type=MESH)
    pl.semaphore_wait(barrier, count - 1 + 2)


def send(src, dst, sems, i, axis, other):
    return pltpu.make_async_remote_copy(
        src_ref=src, dst_ref=dst, send_sem=sems.at[0, i], recv_sem=sems.at[1, i],
        device_id={axis: other}, device_id_type=MESH,
    )


def block(count, out_ref, got_ref, sems, chunk, j):
    me = lax.axis_index("slab")
    other = partner(me, j, count)
    size = out_ref.shape[1] // CHUNKS
    planes = pl.ds(chunk * size, size)
    return other, send(
        out_ref.at[other, planes], got_ref.at[me, planes], sems, chunk * count + j, "slab", other
    )


def main_kernel(
    count, ids_ref, brick_ref, weight_ref, tpl_ref, fixed_ref, vel_ref,
    force_ref, fz_low, fz_high, fy_low, fy_high, vz_low, vz_high, vy_low, vy_high,
    want_ref, there_out, there_got, back_out, back_got, miss_ref, sum_ref,
    tz_low, tz_high, ty_low, ty_high, head_ref, tail_ref,
    want_sems, there_sems, back_sems, halo_sems, own_sem,
):
    z_cells, y_cells, _ = tpl_ref.shape
    me = lax.axis_index("slab")
    pencil = lax.axis_index("pencil")
    depth = there_out.shape[1]
    size = depth // CHUNKS
    keep_below = jnp.where(me == 0, 0.0, 1.0)
    keep_above = jnp.where(me == count - 1, 0.0, 1.0)
    keep_left = jnp.where(pencil == 0, 0.0, 1.0)
    keep_right = jnp.where(pencil == lax.axis_size("pencil") - 1, 0.0, 1.0)
    below, above = ring("slab")
    left, right = ring("pencil")
    z_last, y_last = pl.ds(z_cells - 1, 1), pl.ds(y_cells - 8, 8)
    z_head, y_head = pl.ds(0, 1), pl.ds(0, 8)
    meet(count)

    def want(j):
        other = partner(me, j, count)
        return other, send(ids_ref.at[other], want_ref.at[me], want_sems, j, "slab", other)

    def ask(j, carry):
        want(j)[1].start()
        return carry

    lax.fori_loop(1, count, ask, 0)
    own = pltpu.make_async_copy(ids_ref.at[me], want_ref.at[me], own_sem)
    own.start()
    halos = [
        send(tpl_ref.at[z_last], tz_low, halo_sems, 0, "slab", above),
        send(tpl_ref.at[z_head], tz_high, halo_sems, 1, "slab", below),
        send(vel_ref.at[:, z_last], vz_low, halo_sems, 2, "slab", above),
        send(vel_ref.at[:, z_head], vz_high, halo_sems, 3, "slab", below),
        send(tpl_ref.at[:, y_last], ty_low, halo_sems, 4, "pencil", right),
        send(tpl_ref.at[:, y_head], ty_high, halo_sems, 5, "pencil", left),
        send(vel_ref.at[:, :, y_last], vy_low, halo_sems, 6, "pencil", right),
        send(vel_ref.at[:, :, y_head], vy_high, halo_sems, 7, "pencil", left),
    ]
    own.wait()

    def heard(j, carry):
        want(j)[1].wait()
        return carry

    lax.fori_loop(1, count, heard, 0)

    def there(chunk, carry):
        def start(i, inner):
            other, copy = block(count, there_out, there_got, there_sems, chunk, count - 1 - i)
            pack(tpl_ref, want_ref, None, other, chunk, there_out)
            copy.start()
            return inner

        lax.fori_loop(0, count - 1, start, 0)
        pack(tpl_ref, want_ref, None, me, chunk, there_out)
        return carry

    lax.fori_loop(0, CHUNKS, there, 0)
    for halo in halos:
        halo.start()
    miss_ref[...] = -fixed_ref[...]
    sum_ref[...] = jnp.zeros_like(sum_ref)

    def back(chunk, carry):
        accumulate(there_out, brick_ref, weight_ref, me, chunk, miss_ref)

        def finish(j, inner):
            other, copy = block(count, there_out, there_got, there_sems, chunk, j)
            copy.wait_recv()
            accumulate(there_got, brick_ref, weight_ref, other, chunk, miss_ref)
            return inner

        lax.fori_loop(1, count, finish, 0)

        def start(i, inner):
            other, copy = block(count, back_out, back_got, back_sems, chunk, count - 1 - i)
            pack(miss_ref, brick_ref, weight_ref, other, chunk, back_out)
            copy.start()
            return inner

        lax.fori_loop(0, count - 1, start, 0)
        pack(miss_ref, brick_ref, weight_ref, me, chunk, back_out)
        accumulate(back_out, want_ref, None, me, chunk, sum_ref)
        return carry

    lax.fori_loop(0, CHUNKS, back, 0)
    for halo in halos:
        halo.wait()

    def plane(z):
        here = tpl_ref[z]
        before_z = jnp.where(z == 0, keep_below * tz_low[0], tpl_ref[jnp.maximum(z - 1, 0)])
        after_z = jnp.where(z == z_cells - 1, keep_above * tz_high[0], tpl_ref[jnp.minimum(z + 1, z_cells - 1)])
        half = 0.5 * sum_ref[z]
        before_y, after_y = next_y(here, keep_left * ty_low[z, 7:8], keep_right * ty_high[z, 0:1])
        before_x, after_x = next_x(here)
        for c, slope in enumerate((after_z - before_z, after_y - before_y, after_x - before_x)):
            force = half * slope
            force_ref[c, z] = force
            head_ref[c, pl.ds(z, 1)] = force[0:1]
            tail_ref[c, pl.ds(z, 1)] = force[y_cells - 1:y_cells]

    def end(chunk, carry):
        def finish(j, inner):
            other, copy = block(count, back_out, back_got, back_sems, chunk, j)
            copy.wait_recv()
            accumulate(back_got, want_ref, None, other, chunk, sum_ref)
            return inner

        lax.fori_loop(1, count, finish, 0)
        for part in range(EDGE // depth):

            def step(i, inner, part=part):
                plane(part * depth + chunk * size + i)
                return inner

            lax.fori_loop(0, size, step, 0)
        return carry

    lax.fori_loop(0, CHUNKS, end, 0)
    faces = [
        send(force_ref.at[:, z_last], fz_low, halo_sems, 8, "slab", above),
        send(force_ref.at[:, z_head], fz_high, halo_sems, 9, "slab", below),
        send(tail_ref, fy_low, halo_sems, 10, "pencil", right),
        send(head_ref, fy_high, halo_sems, 11, "pencil", left),
    ]
    for face in faces:
        face.start()

    def drain(chunk, carry):
        def finish(j, inner):
            block(count, there_out, there_got, there_sems, chunk, j)[1].wait_send()
            block(count, back_out, back_got, back_sems, chunk, j)[1].wait_send()
            return inner

        lax.fori_loop(1, count, finish, 0)
        return carry

    lax.fori_loop(0, CHUNKS, drain, 0)
    for face in faces:
        face.wait()


def gradient_kernel(
    vel_ref, vel_before_ref, vel_after_ref, vz_low_ref, vz_high_ref, vy_low_ref, vy_high_ref,
    frc_ref, frc_before_ref, frc_after_ref, fz_low_ref, fz_high_ref, fy_low_ref, fy_high_ref, out_ref,
):
    block = pl.program_id(0)
    blocks = pl.num_programs(0)
    planes = vel_ref.shape[1]

    slab, pencil = lax.axis_index("slab"), lax.axis_index("pencil")
    keep_below = jnp.where(slab == 0, 0.0, 1.0)
    keep_above = jnp.where(slab == lax.axis_size("slab") - 1, 0.0, 1.0)
    keep_left = jnp.where(pencil == 0, 0.0, 1.0)
    keep_right = jnp.where(pencil == lax.axis_size("pencil") - 1, 0.0, 1.0)

    def around(ref, before_ref, after_ref, low_ref, high_ref, y_low, y_high, c, z):
        here = ref[c, z]
        if z == 0:
            below = jnp.where(block == 0, keep_below * low_ref[c, 0], before_ref[c, 0])
        else:
            below = ref[c, z - 1]
        if z == planes - 1:
            above = jnp.where(block == blocks - 1, keep_above * high_ref[c, 0], after_ref[c, 0])
        else:
            above = ref[c, z + 1]
        before_y, after_y = next_y(here, keep_left * y_low, keep_right * y_high)
        before_x, after_x = next_x(here)
        return here, below, above, before_y, after_y, before_x, after_x

    for z in range(planes):
        half = [0.5 * time_step * vel_ref[i, z] for i in range(3)]
        for c in range(3):
            v = around(vel_ref, vel_before_ref, vel_after_ref, vz_low_ref, vz_high_ref, vy_low_ref[c, z, 7:8], vy_high_ref[c, z, 0:1], c, z)
            laplace = 6.0 * v[0] - (((v[1] + v[2]) + (v[3] + v[4])) + (v[5] + v[6]))
            f = around(frc_ref, frc_before_ref, frc_after_ref, fz_low_ref, fz_high_ref, fy_low_ref[c, z:z + 1], fy_high_ref[c, z:z + 1], c, z)
            advect = half[0] * (f[2] - f[1]) + half[1] * (f[4] - f[3]) + half[2] * (f[6] - f[5])
            out_ref[c, z] = smooth_weight * laplace + f[0] - advect


def per_device(template, fixed_image, velocity, src_owner, src_local, weights):
    slab_count = lax.axis_size("slab")
    bricks, picks = src_owner.shape
    capacity = max(2, bricks * picks // slab_count)
    z_cells, y_cells, x_cells = template.shape
    depth = EDGE * capacity // QUADS
    f32, i32 = jnp.float32, jnp.int32
    smem = whole(pltpu.SMEM)
    table = (slab_count, capacity)
    spread = (slab_count, 8, LANES)

    ids, brick_of, slot_weight = pl.pallas_call(
        slots_kernel,
        out_shape=[jax.ShapeDtypeStruct(spread, kind) for kind in (i32, i32, f32)],
        in_specs=[smem] * 3,
        out_specs=[whole()] * 3,
        scratch_shapes=[pltpu.SMEM(table, i32), pltpu.SMEM(table, i32), pltpu.SMEM(table, f32), pltpu.SMEM((slab_count,), i32)],
        name="slots",
    )(src_owner, src_local, weights)

    packed = pltpu.VMEM((slab_count, depth, EDGE, LANES), f32)
    z_face, y_face = (1, y_cells, x_cells), (z_cells, 8, x_cells)
    edge = (3, z_cells, x_cells)
    shapes = [(3,) + template.shape, (3,) + z_face, (3,) + z_face, edge, edge]
    shapes += [(3,) + z_face, (3,) + z_face, (3,) + y_face, (3,) + y_face]
    field = pltpu.VMEM(template.shape, f32)
    block_sems = pltpu.SemaphoreType.DMA((2, CHUNKS * slab_count))
    force, fz_low, fz_high, fy_low, fy_high, vz_low, vz_high, vy_low, vy_high = pl.pallas_call(
        functools.partial(main_kernel, slab_count),
        out_shape=[jax.ShapeDtypeStruct(shape, f32) for shape in shapes],
        in_specs=[whole()] * 5 + [whole(pl.ANY)],
        out_specs=[whole()] + [whole(pl.ANY)] * 8,
        scratch_shapes=[pltpu.VMEM(spread, i32)] + [packed] * 4 + [field] * 2
        + [pltpu.VMEM(z_face, f32)] * 2 + [pltpu.VMEM(y_face, f32)] * 2 + [pltpu.VMEM(edge, f32)] * 2
        + [pltpu.SemaphoreType.DMA((2, slab_count)), block_sems, block_sems, pltpu.SemaphoreType.DMA((2, 12)), pltpu.SemaphoreType.DMA],
        compiler_params=params(collective_id=1, has_side_effects=True),
        name="transport",
    )(ids, brick_of, slot_weight, template, fixed_image, velocity)

    rows = 8
    last = z_cells - 1
    block = (3, rows, y_cells, x_cells)
    plane = (3, 1, y_cells, x_cells)
    z_spec = pl.BlockSpec(plane, lambda z: (0, 0, 0, 0))
    field_specs = [
        pl.BlockSpec(block, lambda z: (0, z, 0, 0)),
        pl.BlockSpec(plane, lambda z: (0, jnp.maximum(z * rows - 1, 0), 0, 0)),
        pl.BlockSpec(plane, lambda z: (0, jnp.minimum(z * rows + rows, last), 0, 0)),
        z_spec,
        z_spec,
    ]
    vy_spec = pl.BlockSpec((3, rows, 8, x_cells), lambda z: (0, z, 0, 0))
    fy_spec = pl.BlockSpec((3, rows, x_cells), lambda z: (0, z, 0))
    return pl.pallas_call(
        gradient_kernel,
        grid=(z_cells // rows,),
        out_shape=jax.ShapeDtypeStruct(velocity.shape, f32),
        in_specs=field_specs + [vy_spec] * 2 + field_specs + [fy_spec] * 2,
        out_specs=pl.BlockSpec(block, lambda z: (0, z, 0, 0)),
        compiler_params=params(),
        name="gradient",
    )(
        velocity, velocity, velocity, vz_low, vz_high, vy_low, vy_high,
        force, force, force, fz_low, fz_high, fy_low, fy_high,
    )


def solution(mesh):
    in_specs = (
        P("slab", "pencil", None),
        P("slab", "pencil", None),
        P(None, "slab", "pencil", None),
        P(("slab", "pencil"), None),
        P(("slab", "pencil"), None),
        P(("slab", "pencil"), None),
    )
    out_specs = P(None, "slab", "pencil", None)
    return jax.shard_map(
        per_device, mesh=mesh, in_specs=in_specs, out_specs=out_specs, check_vma=False
    )
```

```python
import functools

import jax
import jax.numpy as jnp
from jax import lax
from jax.experimental import pallas as pl
from jax.experimental.pallas import tpu as pltpu
from jax.sharding import PartitionSpec as P

EDGE = 32
LANES = 128
QUADS = LANES // EDGE
MESH = pl.DeviceIdType.MESH
LIMIT = 56 * 1024 * 1024
CHUNKS = 4

smooth_weight = 0.1
time_step = 0.5


def whole(memory_space=pltpu.VMEM):
    return pl.BlockSpec(memory_space=memory_space)


def params(**kw):
    return pltpu.CompilerParams(vmem_limit_bytes=LIMIT, **kw)


def lane_quad():
    return lax.broadcasted_iota(jnp.int32, (8, LANES), 1) // EDGE


def slots_kernel(
    owner_ref, local_ref, weight_ref, ids_out, brick_out, weight_out, ids_ref, brick_ref, slot_weight_ref, count_ref
):
    readers, capacity = ids_ref.shape
    picks, bricks = owner_ref.shape

    def clear(i, carry):
        count_ref[i] = 0
        for c in range(capacity):
            ids_ref[i, c] = 0
            brick_ref[i, c] = 0
            slot_weight_ref[i, c] = 0.0
        return carry

    lax.fori_loop(0, readers, clear, 0)

    def place(g, carry):
        for k in range(picks):
            owner = owner_ref[k, g]
            slot = count_ref[owner]
            count_ref[owner] = slot + 1
            ids_ref[owner, slot] = local_ref[k, g]
            brick_ref[owner, slot] = g
            slot_weight_ref[owner, slot] = weight_ref[k, g]
        return carry

    lax.fori_loop(0, bricks, place, 0)
    quad = lane_quad()

    def spread(i, carry):
        for ref, out in ((ids_ref, ids_out), (brick_ref, brick_out), (slot_weight_ref, weight_out)):
            row = jnp.full((8, LANES), ref[i, 0])
            for q in range(1, QUADS):
                row = jnp.where(quad == q, ref[i, q % capacity], row)
            out[i] = row
        return carry

    lax.fori_loop(0, readers, spread, 0)


def masks_of(brick_ref, weight_ref, lead, sign, part, capacity, tile_count):
    quad = lane_quad()
    brick, weight = brick_ref[lead], jnp.ones((8, LANES), jnp.float32)
    if weight_ref is not None:
        weight = weight_ref[lead]
    masks = [[] for _ in range(tile_count)]
    for r in range(QUADS):
        turn = (sign * r % QUADS) * EDGE
        here = pltpu.roll(brick, turn, 1) if turn else brick
        scale = pltpu.roll(weight, turn, 1) if turn and weight_ref is not None else weight
        if capacity < QUADS:
            here = jnp.where((quad - sign * r + QUADS) % QUADS // capacity == part, here, -1)
        for t in range(tile_count):
            masks[t].append(jnp.where(here == t * QUADS + quad, scale, 0.0)[None])
    return masks


def tiles_of(field_ref):
    x_tiles = field_ref.shape[2] // LANES
    return [(y, x) for y in range(field_ref.shape[1] // EDGE) for x in range(x_tiles)]


STEP = 4
ROWS = STEP * EDGE // 8


def pack(field_ref, brick_ref, weight_ref, lead, chunk, out_ref):
    depth = out_ref.shape[1]
    capacity = QUADS * depth // EDGE
    parts = range(QUADS // capacity)
    size = depth // CHUNKS
    tiles = tiles_of(field_ref)
    masks = [masks_of(brick_ref, weight_ref, lead, -1, part, capacity, len(tiles)) for part in parts]

    def body(i, carry):
        z = chunk * size + i * STEP
        sums = [None] * QUADS
        for part in parts:
            for t, (y, x) in enumerate(tiles):
                cells = field_ref[pl.ds(part * depth + z, STEP), pl.ds(y * EDGE, EDGE), pl.ds(x * LANES, LANES)]
                cells = cells.reshape(ROWS, 8, LANES)
                for r in range(QUADS):
                    term = masks[part][t][r] * cells
                    sums[r] = term if sums[r] is None else sums[r] + term
        total = sums[0]
        for r in range(1, QUADS):
            total = total + pltpu.roll(sums[r], r * EDGE, 2)
        out_ref[lead, pl.ds(z, STEP)] = total.reshape(STEP, EDGE, LANES)
        return carry

    lax.fori_loop(0, size // STEP, body, 0)


def accumulate(got_ref, brick_ref, weight_ref, lead, chunk, sum_ref):
    depth = got_ref.shape[1]
    capacity = QUADS * depth // EDGE
    parts = range(QUADS // capacity)
    size = depth // CHUNKS
    tiles = tiles_of(sum_ref)
    masks = [masks_of(brick_ref, weight_ref, lead, 1, part, capacity, len(tiles)) for part in parts]

    def body(i, carry):
        z = chunk * size + i * STEP
        cells = got_ref[lead, pl.ds(z, STEP)].reshape(ROWS, 8, LANES)
        turned = [cells] + [pltpu.roll(cells, r * EDGE, 2) for r in range(1, QUADS)]
        for part in parts:
            for t, (y, x) in enumerate(tiles):
                total = masks[part][t][0] * turned[0]
                for r in range(1, QUADS):
                    total = total + masks[part][t][r] * turned[r]
                at = (pl.ds(part * depth + z, STEP), pl.ds(y * EDGE, EDGE), pl.ds(x * LANES, LANES))
                sum_ref[at] = sum_ref[at] + total.reshape(STEP, EDGE, LANES)
        return carry

    lax.fori_loop(0, size // STEP, body, 0)


def next_x(plane):
    lane = lax.broadcasted_iota(jnp.int32, plane.shape, 1)
    last = plane.shape[1] - 1
    after = jnp.where(lane == last, 0.0, pltpu.roll(plane, last, 1))
    before = jnp.where(lane == 0, 0.0, pltpu.roll(plane, 1, 1))
    return before, after


def next_y(plane, low, high):
    row = lax.broadcasted_iota(jnp.int32, plane.shape, 0)
    last = plane.shape[0] - 1
    after = jnp.where(row == last, high, pltpu.roll(plane, last, 0))
    before = jnp.where(row == 0, low, pltpu.roll(plane, 1, 0))
    return before, after


def partner(me, offset, count):
    other, bit = 0, 1
    while bit < count:
        other = other + ((me // bit + (offset // bit) % 2) % 2) * bit
        bit = bit * 2
    return other


def ring(axis):
    me, count = lax.axis_index(axis), lax.axis_size(axis)
    return (me + count - 1) % count, (me + 1) % count


def meet(count):
    barrier = pltpu.get_barrier_semaphore()
    me = lax.axis_index("slab")

    def greet(j, carry):
        other = partner(me, j, count)
        pl.semaphore_signal(barrier, inc=1, device_id={"slab": other}, device_id_type=MESH)
        return carry

    lax.fori_loop(1, count, greet, 0)
    for other in ring("pencil"):
        pl.semaphore_signal(barrier, inc=1, device_id={"pencil": other}, device_id_type=MESH)
    pl.semaphore_wait(barrier, count - 1 + 2)


def send(src, dst, sems, i, axis, other):
    return pltpu.make_async_remote_copy(
        src_ref=src, dst_ref=dst, send_sem=sems.at[0, i], recv_sem=sems.at[1, i],
        device_id={axis: other}, device_id_type=MESH,
    )


def turn_of(turn):
    return (turn * (CHUNKS - 1)) % CHUNKS


def block(count, out_ref, got_ref, sems, chunk, j):
    me = lax.axis_index("slab")
    other = partner(me, j, count)
    size = out_ref.shape[1] // CHUNKS
    planes = pl.ds(chunk * size, size)
    return other, send(
        out_ref.at[other, planes], got_ref.at[me, planes], sems, chunk * count + j, "slab", other
    )


def main_kernel(
    count, ids_ref, brick_ref, weight_ref, tpl_ref, fixed_ref, vel_ref,
    force_ref, fz_low, fz_high, fy_low, fy_high, vz_low, vz_high, vy_low, vy_high,
    want_ref, there_out, there_got, back_out, back_got, miss_ref, sum_ref, total_ref,
    tz_low, tz_high, ty_low, ty_high, head_ref, tail_ref,
    want_sems, there_sems, back_sems, halo_sems, store_sems, own_sem, fixed_sem,
):
    z_cells, y_cells, _ = tpl_ref.shape
    me = lax.axis_index("slab")
    pencil = lax.axis_index("pencil")
    depth = there_out.shape[1]
    size = depth // CHUNKS
    keep_below = jnp.where(me == 0, 0.0, 1.0)
    keep_above = jnp.where(me == count - 1, 0.0, 1.0)
    keep_left = jnp.where(pencil == 0, 0.0, 1.0)
    keep_right = jnp.where(pencil == lax.axis_size("pencil") - 1, 0.0, 1.0)
    below, above = ring("slab")
    left, right = ring("pencil")
    z_last, y_last = pl.ds(z_cells - 1, 1), pl.ds(y_cells - 8, 8)
    z_head, y_head = pl.ds(0, 1), pl.ds(0, 8)
    fixed = pltpu.make_async_copy(fixed_ref, miss_ref, fixed_sem)
    fixed.start()
    meet(count)

    def want(j):
        other = partner(me, j, count)
        return other, send(ids_ref.at[other], want_ref.at[me], want_sems, j, "slab", other)

    def ask(j, carry):
        want(j)[1].start()
        return carry

    lax.fori_loop(1, count, ask, 0)
    own = pltpu.make_async_copy(ids_ref.at[me], want_ref.at[me], own_sem)
    own.start()
    halos = [
        send(tpl_ref.at[z_last], tz_low, halo_sems, 0, "slab", above),
        send(tpl_ref.at[z_head], tz_high, halo_sems, 1, "slab", below),
        send(vel_ref.at[:, z_last], vz_low, halo_sems, 2, "slab", above),
        send(vel_ref.at[:, z_head], vz_high, halo_sems, 3, "slab", below),
        send(tpl_ref.at[:, y_last], ty_low, halo_sems, 4, "pencil", right),
        send(tpl_ref.at[:, y_head], ty_high, halo_sems, 5, "pencil", left),
        send(vel_ref.at[:, :, y_last], vy_low, halo_sems, 6, "pencil", right),
        send(vel_ref.at[:, :, y_head], vy_high, halo_sems, 7, "pencil", left),
    ]
    for halo in halos:
        halo.start()
    sum_ref[...] = jnp.zeros_like(sum_ref)
    fixed.wait()
    miss_ref[...] = -miss_ref[...]
    own.wait()

    def heard(j, carry):
        want(j)[1].wait()
        return carry

    lax.fori_loop(1, count, heard, 0)

    def there(turn, carry):
        chunk = turn_of(turn)

        def start(i, inner):
            other, copy = block(count, there_out, there_got, there_sems, chunk, count - 1 - i)
            pack(tpl_ref, want_ref, None, other, chunk, there_out)
            copy.start()
            return inner

        lax.fori_loop(0, count - 1, start, 0)
        pack(tpl_ref, want_ref, None, me, chunk, there_out)
        return carry

    lax.fori_loop(0, CHUNKS, there, 0)

    def back(turn, carry):
        chunk = turn_of(turn)
        accumulate(there_out, brick_ref, weight_ref, me, chunk, miss_ref)

        def finish(j, inner):
            other, copy = block(count, there_out, there_got, there_sems, chunk, j)
            copy.wait_recv()
            accumulate(there_got, brick_ref, weight_ref, other, chunk, miss_ref)
            return inner

        lax.fori_loop(1, count, finish, 0)

        def start(i, inner):
            other, copy = block(count, back_out, back_got, back_sems, chunk, count - 1 - i)
            pack(miss_ref, brick_ref, weight_ref, other, chunk, back_out)
            copy.start()
            return inner

        lax.fori_loop(0, count - 1, start, 0)
        pack(miss_ref, brick_ref, weight_ref, me, chunk, back_out)
        accumulate(back_out, want_ref, None, me, chunk, sum_ref)
        return carry

    lax.fori_loop(0, CHUNKS, back, 0)
    for halo in halos:
        halo.wait()

    def plane(z):
        here = tpl_ref[z]
        before_z = jnp.where(z == 0, keep_below * tz_low[0], tpl_ref[jnp.maximum(z - 1, 0)])
        after_z = jnp.where(z == z_cells - 1, keep_above * tz_high[0], tpl_ref[jnp.minimum(z + 1, z_cells - 1)])
        half = 0.5 * sum_ref[z]
        before_y, after_y = next_y(here, keep_left * ty_low[z, 7:8], keep_right * ty_high[z, 0:1])
        before_x, after_x = next_x(here)
        for c, slope in enumerate((after_z - before_z, after_y - before_y, after_x - before_x)):
            force = half * slope
            total_ref[c, z] = force
            head_ref[c, pl.ds(z, 1)] = force[0:1]
            tail_ref[c, pl.ds(z, 1)] = force[y_cells - 1:y_cells]

    def store(chunk, part):
        planes = pl.ds(part * depth + chunk * size, size)
        at = chunk * (EDGE // depth) + part
        return pltpu.make_async_copy(total_ref.at[:, planes], force_ref.at[:, planes], store_sems.at[at])

    def end(turn, carry):
        chunk = turn_of(turn)

        def finish(j, inner):
            other, copy = block(count, back_out, back_got, back_sems, chunk, j)
            copy.wait_recv()
            accumulate(back_got, want_ref, None, other, chunk, sum_ref)
            return inner

        lax.fori_loop(1, count, finish, 0)
        for part in range(EDGE // depth):

            def step(i, inner, part=part):
                plane(part * depth + chunk * size + i)
                return inner

            lax.fori_loop(0, size, step, 0)
            store(chunk, part).start()
        return carry

    lax.fori_loop(0, 2, end, 0)
    faces = [
        send(total_ref.at[:, z_last], fz_low, halo_sems, 8, "slab", above),
        send(total_ref.at[:, z_head], fz_high, halo_sems, 9, "slab", below),
        send(tail_ref, fy_low, halo_sems, 10, "pencil", right),
        send(head_ref, fy_high, halo_sems, 11, "pencil", left),
    ]
    faces[0].start()
    faces[1].start()
    lax.fori_loop(2, CHUNKS, end, 0)
    faces[2].start()
    faces[3].start()

    def drain(chunk, carry):
        def finish(j, inner):
            block(count, there_out, there_got, there_sems, chunk, j)[1].wait_send()
            block(count, back_out, back_got, back_sems, chunk, j)[1].wait_send()
            return inner

        lax.fori_loop(1, count, finish, 0)
        for part in range(EDGE // depth):
            store(chunk, part).wait()
        return carry

    lax.fori_loop(0, CHUNKS, drain, 0)
    for face in faces:
        face.wait()


def gradient_kernel(
    vel_ref, vel_before_ref, vel_after_ref, vz_low_ref, vz_high_ref, vy_low_ref, vy_high_ref,
    frc_ref, frc_before_ref, frc_after_ref, fz_low_ref, fz_high_ref, fy_low_ref, fy_high_ref, out_ref,
):
    block = pl.program_id(0)
    blocks = pl.num_programs(0)
    planes = vel_ref.shape[1]

    slab, pencil = lax.axis_index("slab"), lax.axis_index("pencil")
    keep_below = jnp.where(slab == 0, 0.0, 1.0)
    keep_above = jnp.where(slab == lax.axis_size("slab") - 1, 0.0, 1.0)
    keep_left = jnp.where(pencil == 0, 0.0, 1.0)
    keep_right = jnp.where(pencil == lax.axis_size("pencil") - 1, 0.0, 1.0)

    def around(ref, before_ref, after_ref, low_ref, high_ref, y_low, y_high, c, z):
        here = ref[c, z]
        if z == 0:
            below = jnp.where(block == 0, keep_below * low_ref[c, 0], before_ref[c, 0])
        else:
            below = ref[c, z - 1]
        if z == planes - 1:
            above = jnp.where(block == blocks - 1, keep_above * high_ref[c, 0], after_ref[c, 0])
        else:
            above = ref[c, z + 1]
        before_y, after_y = next_y(here, keep_left * y_low, keep_right * y_high)
        before_x, after_x = next_x(here)
        return here, below, above, before_y, after_y, before_x, after_x

    for z in range(planes):
        half = [0.5 * time_step * vel_ref[i, z] for i in range(3)]
        for c in range(3):
            v = around(vel_ref, vel_before_ref, vel_after_ref, vz_low_ref, vz_high_ref, vy_low_ref[c, z, 7:8], vy_high_ref[c, z, 0:1], c, z)
            laplace = 6.0 * v[0] - (((v[1] + v[2]) + (v[3] + v[4])) + (v[5] + v[6]))
            f = around(frc_ref, frc_before_ref, frc_after_ref, fz_low_ref, fz_high_ref, fy_low_ref[c, z:z + 1], fy_high_ref[c, z:z + 1], c, z)
            advect = half[0] * (f[2] - f[1]) + half[1] * (f[4] - f[3]) + half[2] * (f[6] - f[5])
            out_ref[c, z] = smooth_weight * laplace + f[0] - advect


def per_device(template, fixed_image, velocity, src_owner, src_local, weights):
    slab_count = lax.axis_size("slab")
    bricks, picks = src_owner.shape
    capacity = max(2, bricks * picks // slab_count)
    z_cells, y_cells, x_cells = template.shape
    depth = EDGE * capacity // QUADS
    f32, i32 = jnp.float32, jnp.int32
    smem = whole(pltpu.SMEM)
    table = (slab_count, capacity)
    spread = (slab_count, 8, LANES)

    ids, brick_of, slot_weight = pl.pallas_call(
        slots_kernel,
        out_shape=[jax.ShapeDtypeStruct(spread, kind) for kind in (i32, i32, f32)],
        in_specs=[smem] * 3,
        out_specs=[whole()] * 3,
        scratch_shapes=[pltpu.SMEM(table, i32), pltpu.SMEM(table, i32), pltpu.SMEM(table, f32), pltpu.SMEM((slab_count,), i32)],
        name="slots",
    )(src_owner.T, src_local.T, weights.T)

    packed = pltpu.VMEM((slab_count, depth, EDGE, LANES), f32)
    z_face, y_face = (1, y_cells, x_cells), (z_cells, 8, x_cells)
    edge = (3, z_cells, x_cells)
    shapes = [(3,) + template.shape, (3,) + z_face, (3,) + z_face, edge, edge]
    shapes += [(3,) + z_face, (3,) + z_face, (3,) + y_face, (3,) + y_face]
    field = pltpu.VMEM(template.shape, f32)
    block_sems = pltpu.SemaphoreType.DMA((2, CHUNKS * slab_count))
    force, fz_low, fz_high, fy_low, fy_high, vz_low, vz_high, vy_low, vy_high = pl.pallas_call(
        functools.partial(main_kernel, slab_count),
        out_shape=[jax.ShapeDtypeStruct(shape, f32) for shape in shapes],
        in_specs=[whole()] * 4 + [whole(pl.ANY)] * 2,
        out_specs=[whole(pl.ANY)] * 9,
        scratch_shapes=[pltpu.VMEM(spread, i32)] + [packed] * 4 + [field] * 2 + [pltpu.VMEM((3,) + template.shape, f32)]
        + [pltpu.VMEM(z_face, f32)] * 2 + [pltpu.VMEM(y_face, f32)] * 2 + [pltpu.VMEM(edge, f32)] * 2
        + [pltpu.SemaphoreType.DMA((2, slab_count)), block_sems, block_sems, pltpu.SemaphoreType.DMA((2, 12))]
        + [pltpu.SemaphoreType.DMA((CHUNKS * (EDGE // depth),)), pltpu.SemaphoreType.DMA, pltpu.SemaphoreType.DMA],
        compiler_params=params(collective_id=1, has_side_effects=True),
        name="transport",
    )(ids, brick_of, slot_weight, template, fixed_image, velocity)

    rows = 8
    last = z_cells - 1
    block = (3, rows, y_cells, x_cells)
    plane = (3, 1, y_cells, x_cells)
    z_spec = pl.BlockSpec(plane, lambda z: (0, 0, 0, 0))
    field_specs = [
        pl.BlockSpec(block, lambda z: (0, z, 0, 0)),
        pl.BlockSpec(plane, lambda z: (0, jnp.maximum(z * rows - 1, 0), 0, 0)),
        pl.BlockSpec(plane, lambda z: (0, jnp.minimum(z * rows + rows, last), 0, 0)),
        z_spec,
        z_spec,
    ]
    vy_spec = pl.BlockSpec((3, rows, 8, x_cells), lambda z: (0, z, 0, 0))
    fy_spec = pl.BlockSpec((3, rows, x_cells), lambda z: (0, z, 0))
    return pl.pallas_call(
        gradient_kernel,
        grid=(z_cells // rows,),
        out_shape=jax.ShapeDtypeStruct(velocity.shape, f32),
        in_specs=field_specs + [vy_spec] * 2 + field_specs + [fy_spec] * 2,
        out_specs=pl.BlockSpec(block, lambda z: (0, z, 0, 0)),
        compiler_params=params(),
        name="gradient",
    )(
        velocity, velocity, velocity, vz_low, vz_high, vy_low, vy_high,
        force, force, force, fz_low, fz_high, fy_low, fy_high,
    )


def solution(mesh):
    in_specs = (
        P("slab", "pencil", None),
        P("slab", "pencil", None),
        P(None, "slab", "pencil", None),
        P(("slab", "pencil"), None),
        P(("slab", "pencil"), None),
        P(("slab", "pencil"), None),
    )
    out_specs = P(None, "slab", "pencil", None)
    return jax.shard_map(
        per_device, mesh=mesh, in_specs=in_specs, out_specs=out_specs, check_vma=False
    )
```

```python
import functools

import jax
import jax.numpy as jnp
from jax import lax
from jax.experimental import pallas as pl
from jax.experimental.pallas import tpu as pltpu
from jax.sharding import PartitionSpec as P

EDGE = 32
LANES = 128
QUADS = LANES // EDGE
MESH = pl.DeviceIdType.MESH
LIMIT = 56 * 1024 * 1024
CHUNKS = 4

smooth_weight = 0.1
time_step = 0.5


def whole(memory_space=pltpu.VMEM):
    return pl.BlockSpec(memory_space=memory_space)


def params(**kw):
    return pltpu.CompilerParams(vmem_limit_bytes=LIMIT, **kw)


def lane_quad():
    return lax.broadcasted_iota(jnp.int32, (8, LANES), 1) // EDGE


def slots_kernel(
    owner_ref, local_ref, weight_ref, ids_out, brick_out, weight_out, ids_ref, brick_ref, slot_weight_ref, count_ref
):
    readers, capacity = ids_ref.shape
    picks, bricks = owner_ref.shape

    def clear(i, carry):
        count_ref[i] = 0
        for c in range(capacity):
            ids_ref[i, c] = 0
            brick_ref[i, c] = 0
            slot_weight_ref[i, c] = 0.0
        return carry

    lax.fori_loop(0, readers, clear, 0)

    def place(g, carry):
        for k in range(picks):
            owner = owner_ref[k, g]
            slot = count_ref[owner]
            count_ref[owner] = slot + 1
            ids_ref[owner, slot] = local_ref[k, g]
            brick_ref[owner, slot] = g
            slot_weight_ref[owner, slot] = weight_ref[k, g]
        return carry

    lax.fori_loop(0, bricks, place, 0)
    quad = lane_quad()

    def spread(i, carry):
        for ref, out in ((ids_ref, ids_out), (brick_ref, brick_out), (slot_weight_ref, weight_out)):
            row = jnp.full((8, LANES), ref[i, 0])
            for q in range(1, QUADS):
                row = jnp.where(quad == q, ref[i, q % capacity], row)
            out[i] = row
        return carry

    lax.fori_loop(0, readers, spread, 0)


def masks_of(brick_ref, weight_ref, lead, sign, part, capacity, tile_count):
    quad = lane_quad()
    brick, weight = brick_ref[lead], jnp.ones((8, LANES), jnp.float32)
    if weight_ref is not None:
        weight = weight_ref[lead]
    masks = [[] for _ in range(tile_count)]
    for r in range(QUADS):
        turn = (sign * r % QUADS) * EDGE
        here = pltpu.roll(brick, turn, 1) if turn else brick
        scale = pltpu.roll(weight, turn, 1) if turn and weight_ref is not None else weight
        if capacity < QUADS:
            here = jnp.where((quad - sign * r + QUADS) % QUADS // capacity == part, here, -1)
        for t in range(tile_count):
            masks[t].append(jnp.where(here == t * QUADS + quad, scale, 0.0)[None])
    return masks


def tiles_of(field_ref):
    x_tiles = field_ref.shape[2] // LANES
    return [(y, x) for y in range(field_ref.shape[1] // EDGE) for x in range(x_tiles)]


STEP = 4
ROWS = STEP * EDGE // 8


def pack(field_ref, brick_ref, weight_ref, lead, chunk, out_ref):
    depth = out_ref.shape[1]
    capacity = QUADS * depth // EDGE
    parts = range(QUADS // capacity)
    size = depth // CHUNKS
    tiles = tiles_of(field_ref)
    masks = [masks_of(brick_ref, weight_ref, lead, -1, part, capacity, len(tiles)) for part in parts]

    def body(i, carry):
        z = chunk * size + i * STEP
        sums = [None] * QUADS
        for part in parts:
            for t, (y, x) in enumerate(tiles):
                cells = field_ref[pl.ds(part * depth + z, STEP), pl.ds(y * EDGE, EDGE), pl.ds(x * LANES, LANES)]
                cells = cells.reshape(ROWS, 8, LANES)
                for r in range(QUADS):
                    term = masks[part][t][r] * cells
                    sums[r] = term if sums[r] is None else sums[r] + term
        total = sums[0]
        for r in range(1, QUADS):
            total = total + pltpu.roll(sums[r], r * EDGE, 2)
        out_ref[lead, pl.ds(z, STEP)] = total.reshape(STEP, EDGE, LANES)
        return carry

    lax.fori_loop(0, size // STEP, body, 0)


def accumulate(got_ref, brick_ref, weight_ref, lead, chunk, sum_ref):
    depth = got_ref.shape[1]
    capacity = QUADS * depth // EDGE
    parts = range(QUADS // capacity)
    size = depth // CHUNKS
    tiles = tiles_of(sum_ref)
    masks = [masks_of(brick_ref, weight_ref, lead, 1, part, capacity, len(tiles)) for part in parts]

    def body(i, carry):
        z = chunk * size + i * STEP
        cells = got_ref[lead, pl.ds(z, STEP)].reshape(ROWS, 8, LANES)
        turned = [cells] + [pltpu.roll(cells, r * EDGE, 2) for r in range(1, QUADS)]
        for part in parts:
            for t, (y, x) in enumerate(tiles):
                total = masks[part][t][0] * turned[0]
                for r in range(1, QUADS):
                    total = total + masks[part][t][r] * turned[r]
                at = (pl.ds(part * depth + z, STEP), pl.ds(y * EDGE, EDGE), pl.ds(x * LANES, LANES))
                sum_ref[at] = sum_ref[at] + total.reshape(STEP, EDGE, LANES)
        return carry

    lax.fori_loop(0, size // STEP, body, 0)


def next_x(plane):
    lane = lax.broadcasted_iota(jnp.int32, plane.shape, 1)
    last = plane.shape[1] - 1
    after = jnp.where(lane == last, 0.0, pltpu.roll(plane, last, 1))
    before = jnp.where(lane == 0, 0.0, pltpu.roll(plane, 1, 1))
    return before, after


def next_y(plane, low, high):
    row = lax.broadcasted_iota(jnp.int32, plane.shape, 0)
    last = plane.shape[0] - 1
    after = jnp.where(row == last, high, pltpu.roll(plane, last, 0))
    before = jnp.where(row == 0, low, pltpu.roll(plane, 1, 0))
    return before, after


def partner(me, offset, count):
    other, bit = 0, 1
    while bit < count:
        other = other + ((me // bit + (offset // bit) % 2) % 2) * bit
        bit = bit * 2
    return other


def ring(axis):
    me, count = lax.axis_index(axis), lax.axis_size(axis)
    return (me + count - 1) % count, (me + 1) % count


def meet(count):
    barrier = pltpu.get_barrier_semaphore()
    me = lax.axis_index("slab")

    def greet(j, carry):
        other = partner(me, j, count)
        pl.semaphore_signal(barrier, inc=1, device_id={"slab": other}, device_id_type=MESH)
        return carry

    lax.fori_loop(1, count, greet, 0)
    for other in ring("pencil"):
        pl.semaphore_signal(barrier, inc=1, device_id={"pencil": other}, device_id_type=MESH)
    pl.semaphore_wait(barrier, count - 1 + 2)


def send(src, dst, sems, i, axis, other):
    return pltpu.make_async_remote_copy(
        src_ref=src, dst_ref=dst, send_sem=sems.at[0, i], recv_sem=sems.at[1, i],
        device_id={axis: other}, device_id_type=MESH,
    )


def turn_of(turn):
    return (turn * (CHUNKS - 1)) % CHUNKS


def block(count, out_ref, got_ref, sems, chunk, j):
    me = lax.axis_index("slab")
    other = partner(me, j, count)
    size = out_ref.shape[1] // CHUNKS
    planes = pl.ds(chunk * size, size)
    return other, send(
        out_ref.at[other, planes], got_ref.at[me, planes], sems, chunk * count + j, "slab", other
    )


def main_kernel(
    count, ids_ref, brick_ref, weight_ref, tpl_ref, fixed_ref, vel_ref,
    force_ref, base_ref, fz_low, fz_high, fy_low, fy_high,
    want_ref, there_out, there_got, back_out, back_got, miss_ref, sum_ref, total_ref,
    speed_ref, vz_low, vz_high, vy_low, vy_high,
    tz_low, tz_high, ty_low, ty_high, head_ref, tail_ref,
    want_sems, there_sems, back_sems, halo_sems, store_sems, own_sem, fixed_sem, speed_sem, base_sem,
):
    z_cells, y_cells, _ = tpl_ref.shape
    me = lax.axis_index("slab")
    pencil = lax.axis_index("pencil")
    depth = there_out.shape[1]
    size = depth // CHUNKS
    keep_below = jnp.where(me == 0, 0.0, 1.0)
    keep_above = jnp.where(me == count - 1, 0.0, 1.0)
    keep_left = jnp.where(pencil == 0, 0.0, 1.0)
    keep_right = jnp.where(pencil == lax.axis_size("pencil") - 1, 0.0, 1.0)
    below, above = ring("slab")
    left, right = ring("pencil")
    z_last, y_last = pl.ds(z_cells - 1, 1), pl.ds(y_cells - 8, 8)
    z_head, y_head = pl.ds(0, 1), pl.ds(0, 8)
    fixed = pltpu.make_async_copy(fixed_ref, miss_ref, fixed_sem)
    fixed.start()
    speed = pltpu.make_async_copy(vel_ref, speed_ref, speed_sem)
    speed.start()
    meet(count)

    def want(j):
        other = partner(me, j, count)
        return other, send(ids_ref.at[other], want_ref.at[me], want_sems, j, "slab", other)

    def ask(j, carry):
        want(j)[1].start()
        return carry

    lax.fori_loop(1, count, ask, 0)
    own = pltpu.make_async_copy(ids_ref.at[me], want_ref.at[me], own_sem)
    own.start()
    halos = [
        send(tpl_ref.at[z_last], tz_low, halo_sems, 0, "slab", above),
        send(tpl_ref.at[z_head], tz_high, halo_sems, 1, "slab", below),
        send(vel_ref.at[:, z_last], vz_low, halo_sems, 2, "slab", above),
        send(vel_ref.at[:, z_head], vz_high, halo_sems, 3, "slab", below),
        send(tpl_ref.at[:, y_last], ty_low, halo_sems, 4, "pencil", right),
        send(tpl_ref.at[:, y_head], ty_high, halo_sems, 5, "pencil", left),
        send(vel_ref.at[:, :, y_last], vy_low, halo_sems, 6, "pencil", right),
        send(vel_ref.at[:, :, y_head], vy_high, halo_sems, 7, "pencil", left),
    ]
    for halo in halos:
        halo.start()
    sum_ref[...] = jnp.zeros_like(sum_ref)
    fixed.wait()
    miss_ref[...] = -miss_ref[...]
    own.wait()

    def heard(j, carry):
        want(j)[1].wait()
        return carry

    lax.fori_loop(1, count, heard, 0)

    def there(turn, carry):
        chunk = turn_of(turn)

        def start(i, inner):
            other, copy = block(count, there_out, there_got, there_sems, chunk, count - 1 - i)
            pack(tpl_ref, want_ref, None, other, chunk, there_out)
            copy.start()
            return inner

        lax.fori_loop(0, count - 1, start, 0)
        pack(tpl_ref, want_ref, None, me, chunk, there_out)
        return carry

    lax.fori_loop(0, CHUNKS, there, 0)
    for halo in halos:
        halo.wait()
    speed.wait()

    def smooth(z, carry):
        for c in range(3):
            here = speed_ref[c, z]
            before_z = jnp.where(z == 0, keep_below * vz_low[c, 0], speed_ref[c, jnp.maximum(z - 1, 0)])
            after_z = jnp.where(
                z == z_cells - 1, keep_above * vz_high[c, 0], speed_ref[c, jnp.minimum(z + 1, z_cells - 1)]
            )
            before_y, after_y = next_y(here, keep_left * vy_low[c, z, 7:8], keep_right * vy_high[c, z, 0:1])
            before_x, after_x = next_x(here)
            around = (before_z + after_z) + (before_y + after_y) + (before_x + after_x)
            total_ref[c, z] = smooth_weight * (6.0 * here - around)
        return carry

    lax.fori_loop(0, z_cells, smooth, 0)
    base = pltpu.make_async_copy(total_ref, base_ref, base_sem)
    base.start()

    def back(turn, carry):
        chunk = turn_of(turn)
        accumulate(there_out, brick_ref, weight_ref, me, chunk, miss_ref)

        def finish(j, inner):
            other, copy = block(count, there_out, there_got, there_sems, chunk, j)
            copy.wait_recv()
            accumulate(there_got, brick_ref, weight_ref, other, chunk, miss_ref)
            return inner

        lax.fori_loop(1, count, finish, 0)

        def start(i, inner):
            other, copy = block(count, back_out, back_got, back_sems, chunk, count - 1 - i)
            pack(miss_ref, brick_ref, weight_ref, other, chunk, back_out)
            copy.start()
            return inner

        lax.fori_loop(0, count - 1, start, 0)
        pack(miss_ref, brick_ref, weight_ref, me, chunk, back_out)
        accumulate(back_out, want_ref, None, me, chunk, sum_ref)
        return carry

    lax.fori_loop(0, CHUNKS, back, 0)
    base.wait()

    def plane(z):
        here = tpl_ref[z]
        before_z = jnp.where(z == 0, keep_below * tz_low[0], tpl_ref[jnp.maximum(z - 1, 0)])
        after_z = jnp.where(z == z_cells - 1, keep_above * tz_high[0], tpl_ref[jnp.minimum(z + 1, z_cells - 1)])
        half = 0.5 * sum_ref[z]
        before_y, after_y = next_y(here, keep_left * ty_low[z, 7:8], keep_right * ty_high[z, 0:1])
        before_x, after_x = next_x(here)
        for c, slope in enumerate((after_z - before_z, after_y - before_y, after_x - before_x)):
            force = half * slope
            total_ref[c, z] = force
            head_ref[c, pl.ds(z, 1)] = force[0:1]
            tail_ref[c, pl.ds(z, 1)] = force[y_cells - 1:y_cells]

    def store(chunk, part):
        planes = pl.ds(part * depth + chunk * size, size)
        at = chunk * (EDGE // depth) + part
        return pltpu.make_async_copy(total_ref.at[:, planes], force_ref.at[:, planes], store_sems.at[at])

    def end(turn, carry):
        chunk = turn_of(turn)

        def finish(j, inner):
            other, copy = block(count, back_out, back_got, back_sems, chunk, j)
            copy.wait_recv()
            accumulate(back_got, want_ref, None, other, chunk, sum_ref)
            return inner

        lax.fori_loop(1, count, finish, 0)
        for part in range(EDGE // depth):

            def step(i, inner, part=part):
                plane(part * depth + chunk * size + i)
                return inner

            lax.fori_loop(0, size, step, 0)
            store(chunk, part).start()
        return carry

    lax.fori_loop(0, 2, end, 0)
    faces = [
        send(total_ref.at[:, z_last], fz_low, halo_sems, 8, "slab", above),
        send(total_ref.at[:, z_head], fz_high, halo_sems, 9, "slab", below),
        send(tail_ref, fy_low, halo_sems, 10, "pencil", right),
        send(head_ref, fy_high, halo_sems, 11, "pencil", left),
    ]
    faces[0].start()
    faces[1].start()
    lax.fori_loop(2, CHUNKS, end, 0)
    faces[2].start()
    faces[3].start()

    def drain(chunk, carry):
        def finish(j, inner):
            block(count, there_out, there_got, there_sems, chunk, j)[1].wait_send()
            block(count, back_out, back_got, back_sems, chunk, j)[1].wait_send()
            return inner

        lax.fori_loop(1, count, finish, 0)
        for part in range(EDGE // depth):
            store(chunk, part).wait()
        return carry

    lax.fori_loop(0, CHUNKS, drain, 0)
    for face in faces:
        face.wait()


def gradient_kernel(
    vel_ref, base_ref,
    frc_ref, frc_before_ref, frc_after_ref, fz_low_ref, fz_high_ref, fy_low_ref, fy_high_ref, out_ref,
):
    block = pl.program_id(0)
    blocks = pl.num_programs(0)
    planes = vel_ref.shape[1]

    slab, pencil = lax.axis_index("slab"), lax.axis_index("pencil")
    keep_below = jnp.where(slab == 0, 0.0, 1.0)
    keep_above = jnp.where(slab == lax.axis_size("slab") - 1, 0.0, 1.0)
    keep_left = jnp.where(pencil == 0, 0.0, 1.0)
    keep_right = jnp.where(pencil == lax.axis_size("pencil") - 1, 0.0, 1.0)

    def around(ref, before_ref, after_ref, low_ref, high_ref, y_low, y_high, c, z):
        here = ref[c, z]
        if z == 0:
            below = jnp.where(block == 0, keep_below * low_ref[c, 0], before_ref[c, 0])
        else:
            below = ref[c, z - 1]
        if z == planes - 1:
            above = jnp.where(block == blocks - 1, keep_above * high_ref[c, 0], after_ref[c, 0])
        else:
            above = ref[c, z + 1]
        before_y, after_y = next_y(here, keep_left * y_low, keep_right * y_high)
        before_x, after_x = next_x(here)
        return here, below, above, before_y, after_y, before_x, after_x

    for z in range(planes):
        half = [0.5 * time_step * vel_ref[i, z] for i in range(3)]
        for c in range(3):
            f = around(frc_ref, frc_before_ref, frc_after_ref, fz_low_ref, fz_high_ref, fy_low_ref[c, z:z + 1], fy_high_ref[c, z:z + 1], c, z)
            advect = half[0] * (f[2] - f[1]) + half[1] * (f[4] - f[3]) + half[2] * (f[6] - f[5])
            out_ref[c, z] = base_ref[c, z] + f[0] - advect


def per_device(template, fixed_image, velocity, src_owner, src_local, weights):
    slab_count = lax.axis_size("slab")
    bricks, picks = src_owner.shape
    capacity = max(2, bricks * picks // slab_count)
    z_cells, y_cells, x_cells = template.shape
    depth = EDGE * capacity // QUADS
    f32, i32 = jnp.float32, jnp.int32
    smem = whole(pltpu.SMEM)
    table = (slab_count, capacity)
    spread = (slab_count, 8, LANES)

    ids, brick_of, slot_weight = pl.pallas_call(
        slots_kernel,
        out_shape=[jax.ShapeDtypeStruct(spread, kind) for kind in (i32, i32, f32)],
        in_specs=[smem] * 3,
        out_specs=[whole()] * 3,
        scratch_shapes=[pltpu.SMEM(table, i32), pltpu.SMEM(table, i32), pltpu.SMEM(table, f32), pltpu.SMEM((slab_count,), i32)],
        name="slots",
    )(src_owner.T, src_local.T, weights.T)

    packed = pltpu.VMEM((slab_count, depth, EDGE, LANES), f32)
    z_face, y_face = (1, y_cells, x_cells), (z_cells, 8, x_cells)
    edge = (3, z_cells, x_cells)
    shapes = [(3,) + template.shape, (3,) + template.shape, (3,) + z_face, (3,) + z_face, edge, edge]
    field = pltpu.VMEM(template.shape, f32)
    block_sems = pltpu.SemaphoreType.DMA((2, CHUNKS * slab_count))
    force, base, fz_low, fz_high, fy_low, fy_high = pl.pallas_call(
        functools.partial(main_kernel, slab_count),
        out_shape=[jax.ShapeDtypeStruct(shape, f32) for shape in shapes],
        in_specs=[whole()] * 4 + [whole(pl.ANY)] * 2,
        out_specs=[whole(pl.ANY)] * 6,
        scratch_shapes=[pltpu.VMEM(spread, i32)] + [packed] * 4 + [field] * 2 + [pltpu.VMEM((3,) + template.shape, f32)] * 2
        + [pltpu.VMEM((3,) + z_face, f32)] * 2 + [pltpu.VMEM((3,) + y_face, f32)] * 2
        + [pltpu.VMEM(z_face, f32)] * 2 + [pltpu.VMEM(y_face, f32)] * 2 + [pltpu.VMEM(edge, f32)] * 2
        + [pltpu.SemaphoreType.DMA((2, slab_count)), block_sems, block_sems, pltpu.SemaphoreType.DMA((2, 12))]
        + [pltpu.SemaphoreType.DMA((CHUNKS * (EDGE // depth),)), pltpu.SemaphoreType.DMA] + [pltpu.SemaphoreType.DMA] * 3,
        compiler_params=params(collective_id=1, has_side_effects=True),
        name="transport",
    )(ids, brick_of, slot_weight, template, fixed_image, velocity)

    rows = 8
    last = z_cells - 1
    block = (3, rows, y_cells, x_cells)
    plane = (3, 1, y_cells, x_cells)
    z_spec = pl.BlockSpec(plane, lambda z: (0, 0, 0, 0))
    field_specs = [
        pl.BlockSpec(block, lambda z: (0, z, 0, 0)),
        pl.BlockSpec(plane, lambda z: (0, jnp.maximum(z * rows - 1, 0), 0, 0)),
        pl.BlockSpec(plane, lambda z: (0, jnp.minimum(z * rows + rows, last), 0, 0)),
        z_spec,
        z_spec,
    ]
    fy_spec = pl.BlockSpec((3, rows, x_cells), lambda z: (0, z, 0))
    return pl.pallas_call(
        gradient_kernel,
        grid=(z_cells // rows,),
        out_shape=jax.ShapeDtypeStruct(velocity.shape, f32),
        in_specs=field_specs[:1] * 2 + field_specs + [fy_spec] * 2,
        out_specs=pl.BlockSpec(block, lambda z: (0, z, 0, 0)),
        compiler_params=params(),
        name="gradient",
    )(
        velocity, base,
        force, force, force, fz_low, fz_high, fy_low, fy_high,
    )


def solution(mesh):
    in_specs = (
        P("slab", "pencil", None),
        P("slab", "pencil", None),
        P(None, "slab", "pencil", None),
        P(("slab", "pencil"), None),
        P(("slab", "pencil"), None),
        P(("slab", "pencil"), None),
    )
    out_specs = P(None, "slab", "pencil", None)
    return jax.shard_map(
        per_device, mesh=mesh, in_specs=in_specs, out_specs=out_specs, check_vma=False
    )
```
